256 devices in a mesh: section: 2 (over core), row: 8 (over z), col: 16 (over y, x).
Axes of the slice: x: 4, y: 4, z: 8, core: 2. Of those that a mesh axis runs over, the one named last changes fastest.
Arguments:
- inputs: bfloat16 [2, 1024, 6144], P(None, 'row'), may hold values from -6 to 6
- norm_gain: float32 [2, 6144], P('section'), may hold values from 0.1 to 1.9
- w_in: bfloat16 [2, 8, 16, 8, 128, 128], P('section', 'row', 'col'), may hold values from -0.3125 to 0.3125
- w_in_slot: int32 [2, 8, 16, 8], P('section', 'row', 'col'), may hold values from 0 to 71, as said below
- w_in_count: int32 [2, 8, 16], P('section', 'row', 'col'), may hold values from 2 to 8, as said below
- w_out: bfloat16 [2, 8, 16, 8, 128, 128], P('section', 'row', 'col'), may hold values from -0.15625 to 0.15625
- w_out_slot: int32 [2, 8, 16, 8], P('section', 'row', 'col'), may hold values from 0 to 71, as said below
- w_out_count: int32 [2, 8, 16], P('section', 'row', 'col'), may hold values from 2 to 8, as said below
Outputs:
- phase_outputs: bfloat16 [2, 2, 1024, 6144], P('section', None, 'row', 'col')
The draws below stay inside these ranges and needn't reach their ends.
Inputs may be any that keep to these rules, and one draw needn't show every extreme that they name: `w_in_slot`: positions p = d * 12 + f of a block in its cell's 6 x 12 grid of blocks; distinct within a cell; slots at or beyond the cell's count are ignored. `w_in_count`: used slots are the leading ones; in every phase each grid row has a cell with exactly 8. `w_out_slot`: positions p = d * 12 + f of a block in its cell's 6 x 12 grid of blocks; distinct within a cell; slots at or beyond the cell's count are ignored. `w_out_count`: used slots are the leading ones; in every phase each grid row has a cell with exactly 8.
All inputs are finite; a program needn't handle non-finite values.
Results may differ from the reference program's by a relative error of at most 0.012.
Values may be sent and summed in bfloat16 or wider, within the bound.
No kernel may reach another device: no remote copies, remote signals or barrier semaphores. Data moves between devices by JAX's collectives and lax.ppermute only.
A program may use at most 64 MiB of HBM per device.

```python
import jax
import jax.numpy as jnp
from jax import lax

D = 6144
FF = 24576
BLK = 128
MICRO = 2
SECTIONS = 2
GRID_ROWS = 8
GRID_COLS = 16
MTOK = 1024
DBL = 6
FBL = 12
CELL_BLOCKS = 72
NZ_MAX = 8


def cell_counts(key):
    key_base, key_heavy = jax.random.split(key)
    baseline = jax.random.randint(key_base, (SECTIONS, GRID_ROWS, GRID_COLS), NZ_MAX // 4, NZ_MAX // 2 + 1)
    heavy_col = jax.random.randint(key_heavy, (SECTIONS, GRID_ROWS, 1), 0, GRID_COLS)
    columns = jnp.arange(GRID_COLS, dtype=jnp.int32)[None, None, :]
    return jnp.where(columns == heavy_col, NZ_MAX, baseline).astype(jnp.int32)


def cell_slots(key):
    cell_keys = jax.random.split(key, SECTIONS * GRID_ROWS * GRID_COLS)
    chosen = jax.vmap(lambda single: jax.random.permutation(single, CELL_BLOCKS)[:NZ_MAX])(cell_keys)
    return chosen.reshape(SECTIONS, GRID_ROWS, GRID_COLS, NZ_MAX).astype(jnp.int32)


def draw_w_in_slot(key, part):
    return cell_slots(jax.random.fold_in(key, 21))


def draw_w_in_count(key, part):
    return cell_counts(jax.random.fold_in(key, 11))


def draw_w_out_slot(key, part):
    return cell_slots(jax.random.fold_in(key, 22))


def draw_w_out_count(key, part):
    return cell_counts(jax.random.fold_in(key, 12))


def shard_levels(own_key, extent, cuts, smallest, top_value):
    level, own = 1.0, jax.random.fold_in(own_key, 6)
    for position, parts in cuts:
        heights = jnp.exp(jax.random.uniform(jax.random.fold_in(own, position), (parts,), jnp.float32, smallest / len(cuts), top_value / len(cuts)))
        level = level * jnp.repeat(heights, extent[position] // parts).reshape([-1 if axis == position else 1 for axis in range(len(extent))])
    return level


def gaussian(key, shape, width, limit, pieces=(), kind=jnp.bfloat16):
    values = jax.random.normal(key, shape, jnp.float32) * width
    if len(pieces) > 0:
        values = shard_levels(key, shape, pieces, -0.22, 0.18) * values
    return jnp.clip(values, min=-limit, max=limit).astype(kind)


def setup_inputs(seed: int = 0) -> dict:
    seeds = jax.random.split(jax.random.key(seed), 9)
    inputs = gaussian(seeds[0], (MICRO, MTOK, D), 1.0, 6.0, ((1, 8),))
    norm_gain = jnp.clip(1.0 + 0.18 * jax.random.normal(seeds[1], (SECTIONS, D), jnp.float32), 0.1, 1.9)
    w_in = gaussian(seeds[2], (SECTIONS, GRID_ROWS, GRID_COLS, NZ_MAX, BLK, BLK), (D // 20) ** -0.5, 0.3125, ((0, 2), (1, 8), (2, 16)))
    w_in_slot = draw_w_in_slot(jax.random.fold_in(seeds[8], 71), 0)
    w_in_count = draw_w_in_count(jax.random.fold_in(seeds[8], 71), 0)
    w_out = gaussian(seeds[5], (SECTIONS, GRID_ROWS, GRID_COLS, NZ_MAX, BLK, BLK), (FF // 20) ** -0.5, 0.15625, ((0, 2), (1, 8), (2, 16)))
    w_out_slot = draw_w_out_slot(jax.random.fold_in(seeds[8], 71), 0)
    w_out_count = draw_w_out_count(jax.random.fold_in(seeds[8], 71), 0)
    return {"inputs": inputs, "norm_gain": norm_gain, "w_in": w_in, "w_in_slot": w_in_slot, "w_in_count": w_in_count, "w_out": w_out, "w_out_slot": w_out_slot, "w_out_count": w_out_count}


EPSILON = 1e-05

def feed_forward(x_rows, gain_row, in_blocks, in_slots, in_counts, out_blocks, out_slots, out_counts):
    as_float = x_rows.astype(jnp.float32)
    scaled = as_float * lax.rsqrt(lax.optimization_barrier(jnp.mean(as_float * as_float, axis=1, keepdims=True)) + EPSILON) * gain_row[None, :]
    normed = scaled.astype(jnp.bfloat16)
    token_rows = x_rows.shape[0]
    model_split = normed.reshape(token_rows, D // BLK, BLK)
    slot_range = jnp.arange(NZ_MAX, dtype=jnp.int32)
    col_range = jnp.arange(GRID_COLS, dtype=jnp.int32)
    row_range = jnp.arange(GRID_ROWS, dtype=jnp.int32)

    def hidden_step(running, row_idx):
        slot_ids = in_slots[row_idx].astype(jnp.int32)
        usable = (slot_range[None, :] < in_counts[row_idx][:, None]).astype(jnp.float32)
        model_block = (row_idx * DBL + slot_ids // FBL).astype(jnp.int32)
        hidden_block = (col_range[:, None] * FBL + slot_ids % FBL).astype(jnp.int32)
        chosen = jnp.take(model_split, model_block.reshape(-1), axis=1).astype(jnp.float32)
        weights = in_blocks[row_idx].reshape(-1, BLK, BLK).astype(jnp.float32)
        products = jnp.einsum('mek,ekf->emf', chosen, weights) * usable.reshape(-1, 1, 1)
        return (running + jax.ops.segment_sum(products, hidden_block.reshape(-1), num_segments=FF // BLK), None)
    start_hidden = jnp.zeros((FF // BLK, token_rows, BLK), jnp.float32)
    before, unused = lax.scan(hidden_step, start_hidden, row_range)
    before = jnp.transpose(before, (1, 0, 2)).reshape(token_rows, FF)
    hidden = jax.nn.gelu(before).astype(jnp.bfloat16)
    hidden_split = hidden.reshape(token_rows, FF // BLK, BLK)

    def output_step(running, col_idx):
        slot_ids = out_slots[:, col_idx].astype(jnp.int32)
        usable = (slot_range[None, :] < out_counts[:, col_idx][:, None]).astype(jnp.float32)
        hidden_block = (col_idx * FBL + slot_ids % FBL).astype(jnp.int32)
        model_block = (row_range[:, None] * DBL + slot_ids // FBL).astype(jnp.int32)
        chosen = jnp.take(hidden_split, hidden_block.reshape(-1), axis=1).astype(jnp.float32)
        weights = out_blocks[:, col_idx].reshape(-1, BLK, BLK).astype(jnp.float32)
        products = jnp.einsum('mek,ekf->emf', chosen, weights) * usable.reshape(-1, 1, 1)
        part = jax.ops.segment_sum(products, model_block.reshape(-1), num_segments=D // BLK)
        part = lax.optimization_barrier(part.astype(jnp.bfloat16)).astype(jnp.float32)
        return (running + part, None)
    start_output = jnp.zeros((D // BLK, token_rows, BLK), jnp.float32)
    summed, unused = lax.scan(output_step, start_output, col_range)
    return jnp.transpose(summed, (1, 0, 2)).reshape(token_rows, D)

def reference(inputs, norm_gain, w_in, w_in_slot, w_in_count, w_out, w_out_slot, w_out_count):
    per_phase = [[] for phase_idx in range(SECTIONS)]
    for micro_idx in range(MICRO):
        current = inputs[micro_idx]
        for phase_idx in range(SECTIONS):
            branch = feed_forward(current, norm_gain[phase_idx], w_in[phase_idx], w_in_slot[phase_idx], w_in_count[phase_idx], w_out[phase_idx], w_out_slot[phase_idx], w_out_count[phase_idx])
            current = (current.astype(jnp.float32) + branch).astype(jnp.bfloat16)
            per_phase[phase_idx].append(current)
    return jnp.stack([jnp.stack(outputs_of) for outputs_of in per_phase])
```

```python
import functools

import jax
import jax.numpy as jnp
from jax import lax
from jax.experimental import pallas as pl
from jax.experimental.pallas import tpu as pltpu
from jax.sharding import PartitionSpec as P

EPSILON = 1e-05
BLK = 128
SLOTS = 8
TAIL = 16
GRID_ROWS = 8
SIDE = 4
DBL = 6
FBL = 12
BLOCKS = 48
CHUNK = 3
TOK = 128
WIDTH = CHUNK * BLK


F32 = jnp.float32
BF16 = jnp.bfloat16


def vmem():
    return pl.BlockSpec(memory_space=pltpu.VMEM)


def smem():
    return pl.BlockSpec(memory_space=pltpu.SMEM)


def chunk_of(place_ref, first, second):
    core = place_ref[0]
    return jnp.where(core == 0, second * SIDE + first, first * SIDE + second)


def digit(value):
    return lax.rem(value + 2 * SIDE, SIDE)


def read_meta(cells, meta_vmem, meta_smem):
    for i, cell in enumerate(cells):
        row = cell[SLOTS * BLK : SLOTS * BLK + TAIL, :].astype(F32)
        meta_vmem[i, :, :] = row[0:8, :].astype(jnp.int32)
    pltpu.sync_copy(meta_vmem, meta_smem)


def block_sum(dense, cells, meta_smem, total):
    for i, cell in enumerate(cells):
        for n in range(SLOTS):
            source = meta_smem[i, 0, n]
            target = meta_smem[i, 0, SLOTS + n]
            total[target] += jnp.dot(
                dense[source], cell[n * BLK : (n + 1) * BLK, :], preferred_element_type=F32
            )


def gelu_into(total, hidden):
    for f in range(FBL):
        hidden[f] = jax.nn.gelu(total[f], approximate=True).astype(BF16)


def first_norm_kernel(micro_ref, place_ref, x_ref, gain_ref, normed_ref, own_ref):
    squares = jnp.zeros((TOK, BLK), F32)
    for k in range(BLOCKS):
        part = x_ref[0, :, k * BLK : (k + 1) * BLK].astype(F32)
        squares = squares + part * part
    mean = jnp.sum(squares, axis=1, keepdims=True) / (BLOCKS * BLK)
    scale = lax.rsqrt(mean + EPSILON)
    for k in range(BLOCKS):
        part = x_ref[0, :, k * BLK : (k + 1) * BLK].astype(F32)
        normed_ref[k] = (part * scale * gain_ref[k]).astype(BF16)
    start = pl.multiple_of(place_ref[1] * WIDTH, BLK)
    own_ref[...] = x_ref[0, :, pl.ds(start, WIDTH)]


def first_in_kernel(normed_ref, *refs):
    cells = refs[:GRID_ROWS]
    hidden_ref, total, meta_vmem, meta_smem = refs[GRID_ROWS:]
    read_meta(cells, meta_vmem, meta_smem)
    total[...] = jnp.zeros_like(total)
    block_sum(normed_ref, cells, meta_smem, total)
    gelu_into(total, hidden_ref)


def later_in_kernel(place_ref, gain_ref, *refs):
    bundles = refs[:SIDE]
    cells = refs[SIDE : SIDE + GRID_ROWS]
    hidden_ref, normed, total, meta_vmem, meta_smem = refs[SIDE + GRID_ROWS :]
    read_meta(cells, meta_vmem, meta_smem)
    squares = jnp.zeros((TOK, BLK), F32)
    for d in range(SIDE):
        for e in range(SIDE):
            for q in range(CHUNK):
                part = bundles[d][e, :, q * BLK : (q + 1) * BLK].astype(F32)
                squares = squares + part * part
    mean = jnp.sum(squares, axis=1, keepdims=True) / (BLOCKS * BLK)
    scale = lax.rsqrt(mean + EPSILON)
    for d in range(SIDE):
        for e in range(SIDE):
            chunk = chunk_of(place_ref, digit(place_ref[2] - d), digit(place_ref[3] - e))
            for q in range(CHUNK):
                k = chunk * CHUNK + q
                part = bundles[d][e, :, q * BLK : (q + 1) * BLK].astype(F32)
                normed[k] = (part * scale * gain_ref[k]).astype(BF16)
    total[...] = jnp.zeros_like(total)
    block_sum(normed, cells, meta_smem, total)
    gelu_into(total, hidden_ref)


def out_kernel(place_ref, hidden_ref, *refs):
    cells = refs[:GRID_ROWS]
    sends = refs[GRID_ROWS : GRID_ROWS + SIDE]
    total, meta_vmem, meta_smem = refs[GRID_ROWS + SIDE :]
    read_meta(cells, meta_vmem, meta_smem)
    total[...] = jnp.zeros_like(total)
    block_sum(hidden_ref, cells, meta_smem, total)
    for d in range(SIDE):
        for e in range(SIDE):
            chunk = chunk_of(place_ref, digit(place_ref[2] + d), digit(place_ref[3] + e))
            for q in range(CHUNK):
                sends[d][e, :, q * BLK : (q + 1) * BLK] = total[chunk * CHUNK + q].astype(BF16)


def sum_kernel(own_ref, one_ref, two_ref, three_ref, *sums):
    for e in range(SIDE):
        value = (
            own_ref[e].astype(F32)
            + one_ref[e].astype(F32)
            + two_ref[e].astype(F32)
            + three_ref[e].astype(F32)
        )
        sums[e][...] = value.astype(sums[e].dtype)


def cost(blocks, moved):
    return pl.CostEstimate(flops=blocks * 2 * BLK**3, bytes_accessed=moved, transcendentals=0)


META = [
    pltpu.VMEM((GRID_ROWS, 8, BLK), jnp.int32),
    pltpu.SMEM((GRID_ROWS, 8, BLK), jnp.int32),
]
NORMED = jax.ShapeDtypeStruct((BLOCKS, TOK, BLK), BF16)
HIDDEN = jax.ShapeDtypeStruct((FBL, TOK, BLK), BF16)
BUNDLE = jax.ShapeDtypeStruct((SIDE, TOK, WIDTH), BF16)
PIECE = jax.ShapeDtypeStruct((TOK, WIDTH), BF16)


def first_norm(micro, place, inputs, gain):
    return pl.pallas_call(
        first_norm_kernel,
        grid_spec=pltpu.PrefetchScalarGridSpec(
            num_scalar_prefetch=2,
            grid=(1,),
            in_specs=[
                pl.BlockSpec((1, TOK, BLOCKS * BLK), lambda i, micro, place: (micro[0], 0, 0)),
                pl.BlockSpec((BLOCKS, 1, BLK), lambda i, micro, place: (0, 0, 0)),
            ],
            out_specs=[
                pl.BlockSpec((BLOCKS, TOK, BLK), lambda i, micro, place: (0, 0, 0)),
                pl.BlockSpec((TOK, WIDTH), lambda i, micro, place: (0, 0)),
            ],
        ),
        out_shape=[NORMED, PIECE],
        cost_estimate=cost(1, 6 << 20),
        name="first_norm",
    )(micro, place, inputs, gain)


def first_in(normed, cells):
    return pl.pallas_call(
        first_in_kernel,
        in_specs=[vmem()] * (1 + GRID_ROWS),
        out_specs=vmem(),
        out_shape=HIDDEN,
        scratch_shapes=[pltpu.VMEM((FBL + 1, TOK, BLK), F32)] + META,
        cost_estimate=cost(512, 8 << 20),
        name="first_in",
    )(normed, *cells)


def later_in(place, gain, bundles, cells):
    return pl.pallas_call(
        later_in_kernel,
        in_specs=[smem()] + [vmem()] * (1 + SIDE + GRID_ROWS),
        out_specs=vmem(),
        out_shape=HIDDEN,
        scratch_shapes=[
            pltpu.VMEM((BLOCKS, TOK, BLK), BF16),
            pltpu.VMEM((FBL + 1, TOK, BLK), F32),
        ]
        + META,
        cost_estimate=cost(512, 12 << 20),
        name="later_in",
    )(place, gain, *bundles, *cells)


def project_out(place, hidden, cells):
    return pl.pallas_call(
        out_kernel,
        in_specs=[smem()] + [vmem()] * (1 + GRID_ROWS),
        out_specs=[vmem()] * SIDE,
        out_shape=[BUNDLE] * SIDE,
        scratch_shapes=[pltpu.VMEM((BLOCKS + 1, TOK, BLK), F32)] + META,
        cost_estimate=cost(512, 8 << 20),
        name="project_out",
    )(place, hidden, *cells)


def sum_bundles(bundles):
    return pl.pallas_call(
        sum_kernel,
        in_specs=[vmem()] * SIDE,
        out_specs=[vmem()] * SIDE,
        out_shape=[jax.ShapeDtypeStruct((TOK, WIDTH), F32)] + [PIECE] * (SIDE - 1),
        cost_estimate=cost(0, 2 << 20),
        name="sum_bundles",
    )(*bundles)


def message(blocks, source, target):
    meta = jnp.concatenate([source, target]).astype(BF16)
    tail = jnp.zeros((TAIL, BLK), BF16).at[0, : 2 * SLOTS].set(meta)
    return jnp.concatenate([blocks.reshape(SLOTS * BLK, BLK), tail], axis=0)


def on_rows(value, perm):
    return lax.ppermute(value, ("section", "row"), perm)


def on_cols(value, perm):
    return lax.ppermute(value, ("section", "col"), perm)


SWAP = [(i, (i + GRID_ROWS) % (2 * GRID_ROWS)) for i in range(2 * GRID_ROWS)]
AROUND = [(r, (r + 1) % GRID_ROWS) for r in range(GRID_ROWS)] + [
    (GRID_ROWS + r, GRID_ROWS + (r - 1) % GRID_ROWS) for r in range(GRID_ROWS)
]


def column_shift(first, distance):
    pairs = []
    for core in range(2):
        for y in range(SIDE):
            for x in range(SIDE):
                along_x = (core == 0) == first
                to_y = y if along_x else (y + distance) % SIDE
                to_x = (x + distance) % SIDE if along_x else x
                base = core * SIDE * SIDE
                pairs.append((base + y * SIDE + x, base + to_y * SIDE + to_x))
    return pairs


def ring_gather(cell):
    ring = [cell]
    for step in range(GRID_ROWS // 2):
        ring.append(on_rows(ring[-1], AROUND))
    other = [on_rows(value, SWAP) for value in ring[1 : GRID_ROWS // 2]]
    return ring + other


def reduce_columns(bundles):
    landed = [on_cols(bundles[d], column_shift(True, d)) for d in range(1, SIDE)]
    sums = sum_bundles([bundles[0]] + landed)
    last = [on_cols(sums[e], column_shift(False, e)) for e in range(1, SIDE)]
    return sums[0], last


def gather_columns(piece):
    pieces = [piece] + [on_cols(piece, column_shift(False, e)) for e in range(1, SIDE)]
    bundle = jnp.stack(pieces)
    return [bundle] + [on_cols(bundle, column_shift(True, d)) for d in range(1, SIDE)]


def add_branch(piece, own_sum, last):
    total = own_sum
    for value in last:
        total = total + value.astype(F32)
    return (piece.astype(F32) + total).astype(BF16)


def shards(inputs, norm_gain, w_in, w_in_slot, w_in_count, w_out, w_out_slot, w_out_count):
    core = lax.axis_index("section")
    row = lax.axis_index("row")
    col = lax.axis_index("col")
    y, x = col // SIDE, col % SIDE
    first = jnp.where(core == 0, x, y)
    second = jnp.where(core == 0, y, x)
    place = jnp.stack([core, col, first, second]).astype(jnp.int32)
    micro = jnp.reshape(core, (1,)).astype(jnp.int32)

    slots = jnp.arange(SLOTS, dtype=jnp.int32)
    in_slot, out_slot = w_in_slot.reshape(SLOTS), w_out_slot.reshape(SLOTS)
    in_used = slots < w_in_count.reshape(())
    out_used = slots < w_out_count.reshape(())
    own_in = message(
        w_in, row * DBL + in_slot // FBL, jnp.where(in_used, in_slot % FBL, FBL)
    )
    own_out = message(
        w_out, out_slot % FBL, jnp.where(out_used, row * DBL + out_slot // FBL, BLOCKS)
    )
    other_in = on_rows(own_in, SWAP)
    other_out = on_rows(own_out, SWAP)
    mine = core == 0
    cells_in = [ring_gather(jnp.where(mine, own_in, other_in))]
    cells_out = [ring_gather(jnp.where(mine, own_out, other_out))]
    cells_in.append(ring_gather(jnp.where(mine, other_in, own_in)))
    cells_out.append(ring_gather(jnp.where(mine, other_out, own_out)))

    own_gain = norm_gain.reshape(BLOCKS, 1, BLK)
    other_gain = on_rows(own_gain, SWAP)
    gains = [jnp.where(mine, own_gain, other_gain), jnp.where(mine, other_gain, own_gain)]

    normed, piece = first_norm(micro, place, inputs, gains[0])
    hidden = first_in(normed, cells_in[0])
    own_sum, last = reduce_columns(project_out(place, hidden, cells_out[0]))
    middle = add_branch(piece, own_sum, last)

    bundles = gather_columns(middle)
    hidden = later_in(place, gains[1], bundles, cells_in[1])
    own_sum, last = reduce_columns(project_out(place, hidden, cells_out[1]))
    final = add_branch(middle, own_sum, last)

    to_first = on_rows(middle, SWAP)
    to_second = on_rows(final, SWAP)
    low = jnp.where(mine, middle, to_second)
    high = jnp.where(mine, to_first, final)
    return jnp.stack([low, high])[None]


def solution(mesh):
    placed = (
        P(None, "row", None),
        P("section", None),
        P("section", "row", "col", None, None, None),
        P("section", "row", "col", None),
        P("section", "row", "col"),
        P("section", "row", "col", None, None, None),
        P("section", "row", "col", None),
        P("section", "row", "col"),
    )
    return jax.shard_map(
        shards,
        mesh=mesh,
        in_specs=placed,
        out_specs=P("section", None, "row", "col"),
        check_vma=False,
    )
```

```python
import functools

import jax
import jax.numpy as jnp
from jax import lax
from jax.experimental import pallas as pl
from jax.experimental.pallas import tpu as pltpu
from jax.sharding import PartitionSpec as P


EPSILON = 1e-05
BLK = 128
SLOTS = 8
UNROLL = 4
GRID_ROWS = 8
OFFSETS = (0, -1, -2, -3, -4, 1, 2, 3)
SIDE = 4
DBL = 6
FBL = 12
BLOCKS = 48
CHUNK = 3
TOK = 128
WIDTH = CHUNK * BLK


F32 = jnp.float32
BF16 = jnp.bfloat16


def vmem():
    return pl.BlockSpec(memory_space=pltpu.VMEM)


def smem():
    return pl.BlockSpec(memory_space=pltpu.SMEM)


def chunk_of(place_ref, first, second):
    core = place_ref[0]
    return jnp.where(core == 0, second * SIDE + first, first * SIDE + second)


def digit(value):
    return lax.rem(value + 2 * SIDE, SIDE)


def fetch(cells, offset, weights, sems):
    copies = [
        pltpu.make_async_copy(
            cell.at[pl.ds(offset, SLOTS)], weights.at[pl.ds(i * SLOTS, SLOTS)], sems.at[i]
        )
        for i, cell in enumerate(cells)
    ]
    for copy in copies:
        copy.start()
    return copies


def list_blocks(place_ref, meta_ref, phase, inward, blocks):
    sign = 1 - 2 * place_ref[0]
    used = 0
    for i, offset in enumerate(OFFSETS):
        row = lax.rem(place_ref[4] + sign * offset + 2 * GRID_ROWS, GRID_ROWS)
        base = phase * GRID_ROWS + row
        start = 0 if inward else SLOTS + 1
        for n in range(SLOTS):
            slot = meta_ref[base, start + n]
            model, hid = row * DBL + slot // FBL, lax.rem(slot, FBL)
            blocks[0, used + n] = i * SLOTS + n
            blocks[1, used + n] = model if inward else hid
            blocks[2, used + n] = hid if inward else model
        used = used + meta_ref[base, start + SLOTS]
    for n in range(UNROLL):
        blocks[0, used + n] = 0
        blocks[1, used + n] = 0
        blocks[2, used + n] = FBL if inward else BLOCKS
    return used


def block_sum(dense, weights, blocks, used, total):
    def group(step, carry):
        at = step * UNROLL
        products = [
            jnp.dot(
                dense[blocks[1, at + u]],
                weights[blocks[0, at + u]],
                preferred_element_type=F32,
            )
            for u in range(UNROLL)
        ]
        for u, product in enumerate(products):
            total[blocks[2, at + u]] += product
        return carry

    lax.fori_loop(0, (used + UNROLL - 1) // UNROLL, group, 0)


def gelu_into(total, hidden):
    for f in range(FBL):
        hidden[f] = jax.nn.gelu(total[f], approximate=True).astype(BF16)


def first_norm_kernel(micro_ref, place_ref, x_ref, gain_ref, normed_ref, own_ref):
    squares = jnp.zeros((TOK, BLK), F32)
    for k in range(BLOCKS):
        part = x_ref[0, :, k * BLK : (k + 1) * BLK].astype(F32)
        squares = squares + part * part
    mean = jnp.sum(squares, axis=1, keepdims=True) / (BLOCKS * BLK)
    scale = lax.rsqrt(mean + EPSILON)
    for k in range(BLOCKS):
        part = x_ref[0, :, k * BLK : (k + 1) * BLK].astype(F32)
        normed_ref[k] = (part * scale * gain_ref[k]).astype(BF16)
    start = pl.multiple_of(place_ref[1] * WIDTH, BLK)
    own_ref[...] = x_ref[0, :, pl.ds(start, WIDTH)]


def first_in_kernel(place_ref, meta_ref, normed_ref, *refs):
    cells = refs[:GRID_ROWS]
    hidden_ref, total, weights, blocks, sems = refs[GRID_ROWS:]
    copies = fetch(cells, 0, weights, sems)
    used = list_blocks(place_ref, meta_ref, 0, True, blocks)
    total[...] = jnp.zeros_like(total)
    for copy in copies:
        copy.wait()
    block_sum(normed_ref, weights, blocks, used, total)
    gelu_into(total, hidden_ref)


def later_in_kernel(place_ref, meta_ref, gain_ref, *refs):
    bundles = refs[:SIDE]
    cells = refs[SIDE : SIDE + GRID_ROWS]
    hidden_ref, normed, total, weights, blocks, sems = refs[SIDE + GRID_ROWS :]
    copies = fetch(cells, 0, weights, sems)
    used = list_blocks(place_ref, meta_ref, 1, True, blocks)
    squares = jnp.zeros((TOK, BLK), F32)
    for d in range(SIDE):
        for e in range(SIDE):
            for q in range(CHUNK):
                part = bundles[d][e, :, q * BLK : (q + 1) * BLK].astype(F32)
                squares = squares + part * part
    mean = jnp.sum(squares, axis=1, keepdims=True) / (BLOCKS * BLK)
    scale = lax.rsqrt(mean + EPSILON)
    for d in range(SIDE):
        for e in range(SIDE):
            chunk = chunk_of(place_ref, digit(place_ref[2] - d), digit(place_ref[3] - e))
            for q in range(CHUNK):
                k = chunk * CHUNK + q
                part = bundles[d][e, :, q * BLK : (q + 1) * BLK].astype(F32)
                normed[k] = (part * scale * gain_ref[k]).astype(BF16)
    total[...] = jnp.zeros_like(total)
    for copy in copies:
        copy.wait()
    block_sum(normed, weights, blocks, used, total)
    gelu_into(total, hidden_ref)


def out_kernel(phase, place_ref, meta_ref, hidden_ref, *refs):
    cells = refs[:GRID_ROWS]
    sends = refs[GRID_ROWS : GRID_ROWS + SIDE]
    total, weights, blocks, sems = refs[GRID_ROWS + SIDE :]
    copies = fetch(cells, phase * SLOTS, weights, sems)
    used = list_blocks(place_ref, meta_ref, phase, False, blocks)
    total[...] = jnp.zeros_like(total)
    for copy in copies:
        copy.wait()
    block_sum(hidden_ref, weights, blocks, used, total)
    for d in range(SIDE):
        for e in range(SIDE):
            chunk = chunk_of(place_ref, digit(place_ref[2] + d), digit(place_ref[3] + e))
            for q in range(CHUNK):
                sends[d][e, :, q * BLK : (q + 1) * BLK] = total[chunk * CHUNK + q].astype(BF16)


def sum_kernel(own_ref, one_ref, two_ref, three_ref, *sums):
    for e in range(SIDE):
        value = (
            own_ref[e].astype(F32)
            + one_ref[e].astype(F32)
            + two_ref[e].astype(F32)
            + three_ref[e].astype(F32)
        )
        sums[e][...] = value.astype(sums[e].dtype)


def cost(blocks, moved):
    return pl.CostEstimate(flops=blocks * 2 * BLK**3, bytes_accessed=moved, transcendentals=0)


WORK = [
    pltpu.VMEM((GRID_ROWS * SLOTS, BLK, BLK), BF16),
    pltpu.SMEM((3, GRID_ROWS * SLOTS + 2 * SLOTS), jnp.int32),
    pltpu.SemaphoreType.DMA((GRID_ROWS,)),
]
PARAMS = pltpu.CompilerParams(vmem_limit_bytes=16 << 20)
NORMED = jax.ShapeDtypeStruct((BLOCKS, TOK, BLK), BF16)
HIDDEN = jax.ShapeDtypeStruct((FBL, TOK, BLK), BF16)
BUNDLE = jax.ShapeDtypeStruct((SIDE, TOK, WIDTH), BF16)
PIECE = jax.ShapeDtypeStruct((TOK, WIDTH), BF16)


def first_norm(micro, place, inputs, gain):
    return pl.pallas_call(
        first_norm_kernel,
        grid_spec=pltpu.PrefetchScalarGridSpec(
            num_scalar_prefetch=2,
            grid=(1,),
            in_specs=[
                pl.BlockSpec((1, TOK, BLOCKS * BLK), lambda i, micro, place: (micro[0], 0, 0)),
                pl.BlockSpec((BLOCKS, 1, BLK), lambda i, micro, place: (0, 0, 0)),
            ],
            out_specs=[
                pl.BlockSpec((BLOCKS, TOK, BLK), lambda i, micro, place: (0, 0, 0)),
                pl.BlockSpec((TOK, WIDTH), lambda i, micro, place: (0, 0)),
            ],
        ),
        out_shape=[NORMED, PIECE],
        cost_estimate=cost(1, 6 << 20),
        compiler_params=PARAMS,
        name="first_norm",
    )(micro, place, inputs, gain)


def anywhere():
    return pl.BlockSpec(memory_space=pl.ANY)


def first_in(place, meta, normed, cells):
    return pl.pallas_call(
        first_in_kernel,
        in_specs=[smem(), smem(), vmem()] + [anywhere()] * GRID_ROWS,
        out_specs=vmem(),
        out_shape=HIDDEN,
        scratch_shapes=[pltpu.VMEM((FBL + 1, TOK, BLK), F32)] + WORK,
        cost_estimate=cost(512, 8 << 20),
        compiler_params=PARAMS,
        name="first_in",
    )(place, meta, normed, *cells)


def later_in(place, meta, gain, bundles, cells):
    return pl.pallas_call(
        later_in_kernel,
        in_specs=[smem(), smem()] + [vmem()] * (1 + SIDE) + [anywhere()] * GRID_ROWS,
        out_specs=vmem(),
        out_shape=HIDDEN,
        scratch_shapes=[
            pltpu.VMEM((BLOCKS, TOK, BLK), BF16),
            pltpu.VMEM((FBL + 1, TOK, BLK), F32),
        ]
        + WORK,
        cost_estimate=cost(512, 12 << 20),
        compiler_params=PARAMS,
        name="later_in",
    )(place, meta, gain, *bundles, *cells)


def project_out(phase, place, meta, hidden, cells):
    return pl.pallas_call(
        functools.partial(out_kernel, phase),
        in_specs=[smem(), smem(), vmem()] + [anywhere()] * GRID_ROWS,
        out_specs=[vmem()] * SIDE,
        out_shape=[BUNDLE] * SIDE,
        scratch_shapes=[pltpu.VMEM((BLOCKS + 1, TOK, BLK), F32)] + WORK,
        cost_estimate=cost(512, 8 << 20),
        compiler_params=PARAMS,
        name="project_out",
    )(place, meta, hidden, *cells)


def sum_bundles(bundles):
    return pl.pallas_call(
        sum_kernel,
        in_specs=[vmem()] * SIDE,
        out_specs=[vmem()] * SIDE,
        out_shape=[jax.ShapeDtypeStruct((TOK, WIDTH), F32)] + [PIECE] * (SIDE - 1),
        cost_estimate=cost(0, 2 << 20),
        compiler_params=PARAMS,
        name="sum_bundles",
    )(*bundles)


def on_rows(value, perm):
    return lax.ppermute(value, ("section", "row"), perm)


def on_cols(value, perm):
    return lax.ppermute(value, ("section", "col"), perm)


SWAP = [(i, (i + GRID_ROWS) % (2 * GRID_ROWS)) for i in range(2 * GRID_ROWS)]
AROUND = [(r, (r + 1) % GRID_ROWS) for r in range(GRID_ROWS)] + [
    (GRID_ROWS + r, GRID_ROWS + (r - 1) % GRID_ROWS) for r in range(GRID_ROWS)
]


def column_shift(first, distance):
    pairs = []
    for core in range(2):
        for y in range(SIDE):
            for x in range(SIDE):
                along_x = (core == 0) == first
                to_y = y if along_x else (y + distance) % SIDE
                to_x = (x + distance) % SIDE if along_x else x
                base = core * SIDE * SIDE
                pairs.append((base + y * SIDE + x, base + to_y * SIDE + to_x))
    return pairs


def ring_gather(cell):
    ring = [cell]
    other = []
    for step in range(1, GRID_ROWS // 2 + 1):
        ring.append(on_rows(ring[-1], AROUND))
        if step < GRID_ROWS // 2:
            other.append(on_rows(ring[-1], SWAP))
    return ring + other


def reduce_columns(bundles):
    landed = []
    for d in range(1, SIDE):
        landed.append(on_cols(bundles[d], column_shift(True, d)))
    sums = sum_bundles([bundles[0]] + landed)
    last = []
    for e in range(1, SIDE):
        last.append(on_cols(sums[e], column_shift(False, e)))
    return sums[0], last


def gather_columns(piece):
    pieces = [piece]
    for e in range(1, SIDE):
        pieces.append(on_cols(piece, column_shift(False, e)))
    bundle = jnp.stack(pieces)
    bundles = [bundle]
    for d in range(1, SIDE):
        bundles.append(on_cols(bundle, column_shift(True, d)))
    return bundles


def add_branch(piece, own_sum, last):
    total = own_sum
    for value in last:
        total = total + value.astype(F32)
    return (piece.astype(F32) + total).astype(BF16)


def shards(inputs, norm_gain, w_in, w_in_slot, w_in_count, w_out, w_out_slot, w_out_count):
    core = lax.axis_index("section")
    row = lax.axis_index("row")
    col = lax.axis_index("col")
    y, x = col // SIDE, col % SIDE
    first = jnp.where(core == 0, x, y)
    second = jnp.where(core == 0, y, x)
    place = jnp.stack([core, col, first, second, row]).astype(jnp.int32)
    micro = jnp.reshape(core, (1,)).astype(jnp.int32)

    own_meta = jnp.concatenate(
        [
            w_in_slot.reshape(SLOTS),
            w_in_count.reshape(1),
            w_out_slot.reshape(SLOTS),
            w_out_count.reshape(1),
            jnp.zeros((BLK - 2 * SLOTS - 2,), jnp.int32),
        ]
    )
    meta = lax.all_to_all(
        jnp.broadcast_to(own_meta, (2 * GRID_ROWS, 1, BLK)),
        ("section", "row"),
        0,
        0,
        tiled=True,
    ).reshape(2 * GRID_ROWS, BLK)
    own_in = w_in.reshape(SLOTS, BLK, BLK)
    own_out = w_out.reshape(SLOTS, BLK, BLK)
    other_in = on_rows(own_in, SWAP)
    other_out = on_rows(own_out, SWAP)
    mine = core == 0
    cells_in = ring_gather(jnp.where(mine, own_in, other_in))
    cells_out = ring_gather(jnp.where(mine, own_out, other_out))
    own_in, own_out, other_in, other_out, _ = lax.optimization_barrier(
        (own_in, own_out, other_in, other_out, cells_in[1])
    )
    later_cells = ring_gather(
        jnp.concatenate(
            [jnp.where(mine, other_in, own_in), jnp.where(mine, other_out, own_out)]
        ),
    )

    own_gain = norm_gain.reshape(BLOCKS, 1, BLK)
    other_gain = on_rows(own_gain, SWAP)
    gains = [jnp.where(mine, own_gain, other_gain), jnp.where(mine, other_gain, own_gain)]

    normed, piece = first_norm(micro, place, inputs, gains[0])
    hidden = first_in(place, meta, normed, cells_in)
    bundles = project_out(0, place, meta, hidden, cells_out)
    own_sum, last = reduce_columns(bundles)
    middle = add_branch(piece, own_sum, last)

    bundles = gather_columns(middle)
    hidden = later_in(place, meta, gains[1], bundles, later_cells)
    bundles = project_out(1, place, meta, hidden, later_cells)
    own_sum, last = reduce_columns(bundles)
    final = add_branch(middle, own_sum, last)

    other = on_rows(jnp.where(mine, final, middle), SWAP)
    return jnp.stack([jnp.where(mine, middle, other), jnp.where(mine, other, final)])[None]


def solution(mesh):
    placed = (
        P(None, "row", None),
        P("section", None),
        P("section", "row", "col", None, None, None),
        P("section", "row", "col", None),
        P("section", "row", "col"),
        P("section", "row", "col", None, None, None),
        P("section", "row", "col", None),
        P("section", "row", "col"),
    )

    return jax.shard_map(
        shards,
        mesh=mesh,
        in_specs=placed,
        out_specs=P("section", None, "row", "col"),
        check_vma=False,
    )
```

```python
import functools

import jax
import jax.numpy as jnp
from jax import lax
from jax.experimental import pallas as pl
from jax.experimental.pallas import tpu as pltpu
from jax.sharding import PartitionSpec as P


EPSILON = 1e-05
BLK = 128
SLOTS = 8
UNROLL = 4
GRID_ROWS = 8
OFFSETS = (0, -1, -2, -3, -4, 1, 2, 3)
SIDE = 4
DBL = 6
FBL = 12
BLOCKS = 48
CHUNK = 3
TOK = 128
WIDTH = CHUNK * BLK


F32 = jnp.float32
BF16 = jnp.bfloat16


def vmem():
    return pl.BlockSpec(memory_space=pltpu.VMEM)


def smem():
    return pl.BlockSpec(memory_space=pltpu.SMEM)


def chunk_of(place_ref, first, second):
    core = place_ref[0]
    return jnp.where(core == 0, second * SIDE + first, first * SIDE + second)


def digit(value):
    return lax.rem(value + 2 * SIDE, SIDE)


def fetch(cells, offset, weights, sems):
    size = SLOTS * BLK
    copies = [
        pltpu.make_async_copy(
            cell.at[pl.ds(offset, size)], weights.at[pl.ds(i * size, size)], sems.at[i]
        )
        for i, cell in enumerate(cells)
    ]
    for copy in copies:
        copy.start()
    return copies


def list_blocks(place_ref, meta_ref, phase, inward, blocks):
    sign = 1 - 2 * place_ref[0]
    start = 0 if inward else SLOTS + 1
    used = 0
    for i, offset in enumerate(OFFSETS):
        row = lax.rem(place_ref[4] + sign * offset + 2 * GRID_ROWS, GRID_ROWS)
        base = phase * GRID_ROWS + row
        for n in range(SLOTS):
            slot = meta_ref[base, start + n]
            model, hid = row * DBL + slot // FBL, lax.rem(slot, FBL)
            blocks[0, used + n] = i * SLOTS + n
            blocks[1, used + n] = model if inward else hid
            blocks[2, used + n] = hid if inward else model
        used = used + meta_ref[base, start + SLOTS]
    for n in range(UNROLL):
        blocks[0, used + n] = 0
        blocks[1, used + n] = 0
        blocks[2, used + n] = FBL if inward else BLOCKS
    return used


def block_sum(dense, weights, blocks, used, total):
    def group(step, carry):
        at = step * UNROLL
        products = [
            jnp.dot(
                dense[blocks[1, at + u]],
                weights[pl.ds(pl.multiple_of(blocks[0, at + u] * BLK, BLK), BLK), :],
                preferred_element_type=F32,
            )
            for u in range(UNROLL)
        ]
        for u, product in enumerate(products):
            total[blocks[2, at + u]] += product
        return carry

    lax.fori_loop(0, (used + UNROLL - 1) // UNROLL, group, 0)


def gelu_into(total, hidden):
    for f in range(FBL):
        hidden[f] = jax.nn.gelu(total[f], approximate=True).astype(BF16)


def first_norm_kernel(micro_ref, place_ref, x_ref, gain_ref, normed_ref, own_ref):
    squares = jnp.zeros((TOK, BLK), F32)
    for k in range(BLOCKS):
        part = x_ref[0, :, k * BLK : (k + 1) * BLK].astype(F32)
        squares = squares + part * part
    mean = jnp.sum(squares, axis=1, keepdims=True) / (BLOCKS * BLK)
    scale = lax.rsqrt(mean + EPSILON)
    for k in range(BLOCKS):
        part = x_ref[0, :, k * BLK : (k + 1) * BLK].astype(F32)
        normed_ref[k] = (part * scale * gain_ref[k]).astype(BF16)
    for e in range(SIDE):
        start = pl.multiple_of(chunk_of(place_ref, place_ref[2], e) * WIDTH, BLK)
        own_ref[e] = x_ref[0, :, pl.ds(start, WIDTH)]


def first_in_kernel(place_ref, meta_ref, normed_ref, *refs):
    cells = refs[:GRID_ROWS]
    hidden_ref, total, weights, blocks, sems = refs[GRID_ROWS:]
    copies = fetch(cells, 0, weights, sems)
    used = list_blocks(place_ref, meta_ref, 0, True, blocks)
    total[...] = jnp.zeros_like(total)
    for copy in copies:
        copy.wait()
    block_sum(normed_ref, weights, blocks, used, total)
    gelu_into(total, hidden_ref)


def later_in_kernel(place_ref, meta_ref, gain_ref, *refs):
    bundles = refs[:SIDE]
    cells = refs[SIDE : SIDE + GRID_ROWS]
    hidden_ref, normed, total, weights, blocks, sems = refs[SIDE + GRID_ROWS :]
    copies = fetch(cells, 0, weights, sems)
    used = list_blocks(place_ref, meta_ref, 1, True, blocks)
    squares = jnp.zeros((TOK, BLK), F32)
    for d in range(SIDE):
        for e in range(SIDE):
            for q in range(CHUNK):
                part = bundles[d][e, :, q * BLK : (q + 1) * BLK].astype(F32)
                squares = squares + part * part
    mean = jnp.sum(squares, axis=1, keepdims=True) / (BLOCKS * BLK)
    scale = lax.rsqrt(mean + EPSILON)
    for d in range(SIDE):
        for e in range(SIDE):
            chunk = chunk_of(place_ref, digit(place_ref[2] - d), e)
            for q in range(CHUNK):
                k = chunk * CHUNK + q
                part = bundles[d][e, :, q * BLK : (q + 1) * BLK].astype(F32)
                normed[k] = (part * scale * gain_ref[k]).astype(BF16)
    total[...] = jnp.zeros_like(total)
    for copy in copies:
        copy.wait()
    block_sum(normed, weights, blocks, used, total)
    gelu_into(total, hidden_ref)


def out_kernel(phase, place_ref, meta_ref, hidden_ref, *refs):
    cells = refs[:GRID_ROWS]
    sends = refs[GRID_ROWS : GRID_ROWS + SIDE]
    total, weights, blocks, sems = refs[GRID_ROWS + SIDE :]
    copies = fetch(cells, phase * SLOTS * BLK, weights, sems)
    used = list_blocks(place_ref, meta_ref, phase, False, blocks)
    total[...] = jnp.zeros_like(total)
    for copy in copies:
        copy.wait()
    block_sum(hidden_ref, weights, blocks, used, total)
    for d in range(SIDE):
        for e in range(SIDE):
            chunk = chunk_of(place_ref, digit(place_ref[2] + d), e)
            for q in range(CHUNK):
                sends[d][e, :, q * BLK : (q + 1) * BLK] = total[chunk * CHUNK + q].astype(BF16)


def sum_of(refs, index):
    value = refs[0][index].astype(F32)
    for ref in refs[1:]:
        value = value + ref[index].astype(F32)
    return value


def whole_sum_kernel(*refs):
    for e in range(SIDE):
        refs[-1][e] = sum_of(refs[:-1], e).astype(BF16)


def merge_kernel(place_ref, *refs):
    bundle_ref, piece_ref = refs[-2:]
    for e in range(SIDE):
        bundle_ref[e] = sum_of(refs[:-2], e).astype(BF16)
    piece_ref[...] = bundle_ref[place_ref[3]]


def piece_sum_kernel(place_ref, *refs):
    for e, piece in enumerate(refs[SIDE:]):
        piece[...] = sum_of(refs[:SIDE], digit(place_ref[3] + e)).astype(piece.dtype)


def cost(blocks, moved):
    return pl.CostEstimate(flops=blocks * 2 * BLK**3, bytes_accessed=moved, transcendentals=0)


WORK = [
    pltpu.VMEM((GRID_ROWS * SLOTS * BLK, BLK), BF16),
    pltpu.SMEM((3, GRID_ROWS * SLOTS + 2 * SLOTS), jnp.int32),
    pltpu.SemaphoreType.DMA((GRID_ROWS,)),
]
PARAMS = pltpu.CompilerParams(vmem_limit_bytes=16 << 20)
NORMED = jax.ShapeDtypeStruct((BLOCKS, TOK, BLK), BF16)
HIDDEN = jax.ShapeDtypeStruct((FBL, TOK, BLK), BF16)
BUNDLE = jax.ShapeDtypeStruct((SIDE, TOK, WIDTH), BF16)
PIECE = jax.ShapeDtypeStruct((TOK, WIDTH), BF16)


def first_norm(micro, place, inputs, gain):
    return pl.pallas_call(
        first_norm_kernel,
        grid_spec=pltpu.PrefetchScalarGridSpec(
            num_scalar_prefetch=2,
            grid=(1,),
            in_specs=[
                pl.BlockSpec((1, TOK, BLOCKS * BLK), lambda i, micro, place: (micro[0], 0, 0)),
                pl.BlockSpec((BLOCKS, 1, BLK), lambda i, micro, place: (0, 0, 0)),
            ],
            out_specs=[
                pl.BlockSpec((BLOCKS, TOK, BLK), lambda i, micro, place: (0, 0, 0)),
                pl.BlockSpec((SIDE, TOK, WIDTH), lambda i, micro, place: (0, 0, 0)),
            ],
        ),
        out_shape=[NORMED, BUNDLE],
        cost_estimate=cost(1, 6 << 20),
        compiler_params=PARAMS,
        name="first_norm",
    )(micro, place, inputs, gain)


def anywhere():
    return pl.BlockSpec(memory_space=pl.ANY)


def first_in(place, meta, normed, cells):
    return pl.pallas_call(
        first_in_kernel,
        in_specs=[smem(), smem(), vmem()] + [anywhere()] * GRID_ROWS,
        out_specs=vmem(),
        out_shape=HIDDEN,
        scratch_shapes=[pltpu.VMEM((FBL + 1, TOK, BLK), F32)] + WORK,
        cost_estimate=cost(512, 8 << 20),
        compiler_params=PARAMS,
        name="first_in",
    )(place, meta, normed, *cells)


def later_in(place, meta, gain, bundles, cells):
    return pl.pallas_call(
        later_in_kernel,
        in_specs=[smem(), smem()] + [vmem()] * (1 + SIDE) + [anywhere()] * GRID_ROWS,
        out_specs=vmem(),
        out_shape=HIDDEN,
        scratch_shapes=[
            pltpu.VMEM((BLOCKS, TOK, BLK), BF16),
            pltpu.VMEM((FBL + 1, TOK, BLK), F32),
        ]
        + WORK,
        cost_estimate=cost(512, 12 << 20),
        compiler_params=PARAMS,
        name="later_in",
    )(place, meta, gain, *bundles, *cells)


def project_out(phase, place, meta, hidden, cells):
    return pl.pallas_call(
        functools.partial(out_kernel, phase),
        in_specs=[smem(), smem(), vmem()] + [anywhere()] * GRID_ROWS,
        out_specs=[vmem()] * SIDE,
        out_shape=[BUNDLE] * SIDE,
        scratch_shapes=[pltpu.VMEM((BLOCKS + 1, TOK, BLK), F32)] + WORK,
        cost_estimate=cost(512, 8 << 20),
        compiler_params=PARAMS,
        name="project_out",
    )(place, meta, hidden, *cells)


def add_up(kernel, place, bundles, outs):
    return pl.pallas_call(
        kernel,
        in_specs=([smem()] if place is not None else []) + [vmem()] * len(bundles),
        out_specs=[vmem()] * len(outs),
        out_shape=outs,
        cost_estimate=cost(0, 2 << 20),
        compiler_params=PARAMS,
    )(*([place] if place is not None else []), *bundles)


def on_rows(value, perm):
    return lax.ppermute(value, ("section", "row"), perm)


def on_cols(value, perm):
    return lax.ppermute(value, ("section", "col"), perm)


SWAP = [(i, (i + GRID_ROWS) % (2 * GRID_ROWS)) for i in range(2 * GRID_ROWS)]
AROUND = [(r, (r + 1) % GRID_ROWS) for r in range(GRID_ROWS)] + [
    (GRID_ROWS + r, GRID_ROWS + (r - 1) % GRID_ROWS) for r in range(GRID_ROWS)
]


def column_shift(first, distance):
    pairs = []
    for core in range(2):
        for y in range(SIDE):
            for x in range(SIDE):
                along_x = (core == 0) == first
                to_y = y if along_x else (y + distance) % SIDE
                to_x = (x + distance) % SIDE if along_x else x
                base = core * SIDE * SIDE
                pairs.append((base + y * SIDE + x, base + to_y * SIDE + to_x))
    return pairs


def ring_gather(cell):
    ring = [cell]
    other = []
    for step in range(1, GRID_ROWS // 2 + 1):
        ring.append(on_rows(ring[-1], AROUND))
        if step < GRID_ROWS // 2:
            other.append(on_rows(ring[-1], SWAP))
    return ring + other


def spread(values, first):
    landed = []
    for d in range(1, SIDE):
        value = values[d] if isinstance(values, (list, tuple)) else values
        landed.append(on_cols(value, column_shift(first, d)))
    return landed


def shards(inputs, norm_gain, w_in, w_in_slot, w_in_count, w_out, w_out_slot, w_out_count):
    core = lax.axis_index("section")
    row = lax.axis_index("row")
    col = lax.axis_index("col")
    y, x = col // SIDE, col % SIDE
    first = jnp.where(core == 0, x, y)
    second = jnp.where(core == 0, y, x)
    place = jnp.stack([core, col, first, second, row]).astype(jnp.int32)
    micro = jnp.reshape(core, (1,)).astype(jnp.int32)

    own_meta = jnp.concatenate(
        [
            w_in_slot.reshape(SLOTS),
            w_in_count.reshape(1),
            w_out_slot.reshape(SLOTS),
            w_out_count.reshape(1),
            jnp.zeros((BLK - 2 * SLOTS - 2,), jnp.int32),
        ]
    )
    meta = lax.all_to_all(
        jnp.broadcast_to(own_meta, (2 * GRID_ROWS, 1, BLK)),
        ("section", "row"),
        0,
        0,
        tiled=True,
    ).reshape(2 * GRID_ROWS, BLK)
    own_in = w_in.reshape(SLOTS * BLK, BLK)
    own_out = w_out.reshape(SLOTS * BLK, BLK)
    own_gain = norm_gain.reshape(BLOCKS, 1, BLK)
    other_in = on_rows(own_in, SWAP)
    other_out = on_rows(own_out, SWAP)
    other_gain = on_rows(own_gain, SWAP)
    mine = core == 0
    cells_in = ring_gather(jnp.where(mine, own_in, other_in))
    cells_out = ring_gather(jnp.where(mine, own_out, other_out))
    own_in, own_out, other_in, other_out, _ = lax.optimization_barrier(
        (own_in, own_out, other_in, other_out, cells_in[2])
    )
    later_cells = ring_gather(
        jnp.concatenate(
            [jnp.where(mine, other_in, own_in), jnp.where(mine, other_out, own_out)]
        ),
    )
    gains = [jnp.where(mine, own_gain, other_gain), jnp.where(mine, other_gain, own_gain)]

    normed, own_x = first_norm(micro, place, inputs, gains[0])
    hidden = first_in(place, meta, normed, cells_in)
    bundles = project_out(0, place, meta, hidden, cells_out)
    landed = spread(bundles, True)
    sums = add_up(whole_sum_kernel, None, [bundles[0]] + landed, [BUNDLE])[0]
    landed = spread(sums, False)
    middle, piece = add_up(merge_kernel, place, [own_x, sums] + landed, [BUNDLE, PIECE])

    bundles = [middle] + spread(middle, True)
    hidden = later_in(place, meta, gains[1], bundles, later_cells)
    bundles = project_out(1, place, meta, hidden, later_cells)
    landed = spread(bundles, True)
    sums = add_up(
        piece_sum_kernel,
        place,
        [bundles[0]] + landed,
        [jax.ShapeDtypeStruct((TOK, WIDTH), F32)] + [PIECE] * (SIDE - 1),
    )
    total = sums[0]
    for value in spread(sums, False):
        total = total + value.astype(F32)
    final = (piece.astype(F32) + total).astype(BF16)

    other = on_rows(jnp.where(mine, final, piece), SWAP)
    return jnp.stack([jnp.where(mine, piece, other), jnp.where(mine, other, final)])[None]


def solution(mesh):
    placed = (
        P(None, "row", None),
        P("section", None),
        P("section", "row", "col", None, None, None),
        P("section", "row", "col", None),
        P("section", "row", "col"),
        P("section", "row", "col", None, None, None),
        P("section", "row", "col", None),
        P("section", "row", "col"),
    )

    return jax.shard_map(
        shards,
        mesh=mesh,
        in_specs=placed,
        out_specs=P("section", None, "row", "col"),
        check_vma=False,
    )
```

```python
import functools

import jax
import jax.numpy as jnp
from jax import lax
from jax.experimental import pallas as pl
from jax.experimental.pallas import tpu as pltpu
from jax.sharding import PartitionSpec as P


EPSILON = 1e-05
BLK = 128
SLOTS = 8
UNROLL = 4
GRID_ROWS = 8
OFFSETS = (0, -1, -2, -3, -4, 1, 2, 3)
SIDE = 4
DBL = 6
FBL = 12
BLOCKS = 48
CHUNK = 3
TOK = 128
WIDTH = CHUNK * BLK


F32 = jnp.float32
BF16 = jnp.bfloat16


def vmem():
    return pl.BlockSpec(memory_space=pltpu.VMEM)


def smem():
    return pl.BlockSpec(memory_space=pltpu.SMEM)


def chunk_of(place_ref, first, second):
    core = place_ref[0]
    return jnp.where(core == 0, second * SIDE + first, first * SIDE + second)


def digit(value):
    return lax.rem(value + 2 * SIDE, SIDE)


def fetch(cells, offset, weights, sems):
    size = SLOTS * BLK
    copies = [
        pltpu.make_async_copy(
            cell.at[pl.ds(offset, size)], weights.at[pl.ds(i * size, size)], sems.at[i]
        )
        for i, cell in enumerate(cells)
    ]
    for copy in copies:
        copy.start()
    return copies


def list_blocks(place_ref, meta_ref, phase, inward, blocks):
    sign = 1 - 2 * place_ref[0]
    start = 0 if inward else SLOTS + 1
    used = 0
    for i, offset in enumerate(OFFSETS):
        row = lax.rem(place_ref[4] + sign * offset + 2 * GRID_ROWS, GRID_ROWS)
        base = phase * GRID_ROWS + row
        for n in range(SLOTS):
            slot = meta_ref[base, start + n]
            model, hid = row * DBL + slot // FBL, lax.rem(slot, FBL)
            blocks[0, used + n] = i * SLOTS + n
            blocks[1, used + n] = model if inward else hid
            blocks[2, used + n] = hid if inward else model
        used = used + meta_ref[base, start + SLOTS]
    for n in range(UNROLL):
        blocks[0, used + n] = 0
        blocks[1, used + n] = 0
        blocks[2, used + n] = FBL if inward else BLOCKS
    return used


def block_sum(dense, weights, blocks, used, total):
    def group(step, carry):
        at = step * UNROLL
        products = [
            jnp.dot(
                dense[blocks[1, at + u]],
                weights[pl.ds(pl.multiple_of(blocks[0, at + u] * BLK, BLK), BLK), :],
                preferred_element_type=F32,
            )
            for u in range(UNROLL)
        ]
        for u, product in enumerate(products):
            total[blocks[2, at + u]] += product
        return carry

    lax.fori_loop(0, (used + UNROLL - 1) // UNROLL, group, 0)


def gelu_into(total, hidden):
    for f in range(FBL):
        hidden[f] = jax.nn.gelu(total[f], approximate=True).astype(BF16)


def first_norm_kernel(micro_ref, place_ref, x_ref, gain_ref, normed_ref, own_ref):
    squares = jnp.zeros((TOK, BLK), F32)
    for k in range(BLOCKS):
        part = x_ref[0, :, k * BLK : (k + 1) * BLK].astype(F32)
        squares = squares + part * part
    mean = jnp.sum(squares, axis=1, keepdims=True) / (BLOCKS * BLK)
    scale = lax.rsqrt(mean + EPSILON)
    for k in range(BLOCKS):
        part = x_ref[0, :, k * BLK : (k + 1) * BLK].astype(F32)
        normed_ref[k] = (part * scale * gain_ref[k]).astype(BF16)
    for e in range(SIDE):
        start = pl.multiple_of(chunk_of(place_ref, place_ref[2], e) * WIDTH, BLK)
        own_ref[e] = x_ref[0, :, pl.ds(start, WIDTH)]


def first_in_kernel(place_ref, meta_ref, normed_ref, *refs):
    cells = refs[:GRID_ROWS]
    hidden_ref, total, weights, blocks, sems = refs[GRID_ROWS:]
    copies = fetch(cells, 0, weights, sems)
    used = list_blocks(place_ref, meta_ref, 0, True, blocks)
    total[...] = jnp.zeros_like(total)
    for copy in copies:
        copy.wait()
    block_sum(normed_ref, weights, blocks, used, total)
    gelu_into(total, hidden_ref)


def later_in_kernel(place_ref, meta_ref, gain_ref, *refs):
    bundles = refs[:SIDE]
    cells = refs[SIDE : SIDE + GRID_ROWS]
    hidden_ref, normed, total, weights, blocks, sems = refs[SIDE + GRID_ROWS :]
    copies = fetch(cells, 0, weights, sems)
    used = list_blocks(place_ref, meta_ref, 1, True, blocks)
    squares = jnp.zeros((TOK, BLK), F32)
    for d in range(SIDE):
        for e in range(SIDE):
            for q in range(CHUNK):
                part = bundles[d][e, :, q * BLK : (q + 1) * BLK].astype(F32)
                squares = squares + part * part
    mean = jnp.sum(squares, axis=1, keepdims=True) / (BLOCKS * BLK)
    scale = lax.rsqrt(mean + EPSILON)
    for d in range(SIDE):
        for e in range(SIDE):
            chunk = chunk_of(place_ref, digit(place_ref[2] - d), e)
            for q in range(CHUNK):
                k = chunk * CHUNK + q
                part = bundles[d][e, :, q * BLK : (q + 1) * BLK].astype(F32)
                normed[k] = (part * scale * gain_ref[k]).astype(BF16)
    total[...] = jnp.zeros_like(total)
    for copy in copies:
        copy.wait()
    block_sum(normed, weights, blocks, used, total)
    gelu_into(total, hidden_ref)


def out_kernel(phase, place_ref, meta_ref, hidden_ref, *refs):
    cells = refs[:GRID_ROWS]
    sends = refs[GRID_ROWS : GRID_ROWS + SIDE]
    total, weights, blocks, sems = refs[GRID_ROWS + SIDE :]
    copies = fetch(cells, phase * SLOTS * BLK, weights, sems)
    used = list_blocks(place_ref, meta_ref, phase, False, blocks)
    total[...] = jnp.zeros_like(total)
    for copy in copies:
        copy.wait()
    block_sum(hidden_ref, weights, blocks, used, total)
    for d in range(SIDE):
        for e in range(SIDE):
            chunk = chunk_of(place_ref, digit(place_ref[2] + d), e)
            for q in range(CHUNK):
                sends[d][e, :, q * BLK : (q + 1) * BLK] = total[chunk * CHUNK + q].astype(BF16)


def sum_of(refs, index):
    value = refs[0][index].astype(F32)
    for ref in refs[1:]:
        value = value + ref[index].astype(F32)
    return value


def whole_sum_kernel(*refs):
    for e in range(SIDE):
        refs[-1][e] = sum_of(refs[:-1], e).astype(BF16)


def merge_kernel(place_ref, *refs):
    bundle_ref, piece_ref = refs[-2:]
    for e in range(SIDE):
        bundle_ref[e] = sum_of(refs[:-2], e).astype(BF16)
    piece_ref[...] = bundle_ref[place_ref[3]]


def cost(blocks, moved):
    return pl.CostEstimate(flops=blocks * 2 * BLK**3, bytes_accessed=moved, transcendentals=0)


WORK = [
    pltpu.VMEM((GRID_ROWS * SLOTS * BLK, BLK), BF16),
    pltpu.SMEM((3, GRID_ROWS * SLOTS + 2 * SLOTS), jnp.int32),
    pltpu.SemaphoreType.DMA((GRID_ROWS,)),
]
PARAMS = pltpu.CompilerParams(vmem_limit_bytes=16 << 20)
NORMED = jax.ShapeDtypeStruct((BLOCKS, TOK, BLK), BF16)
HIDDEN = jax.ShapeDtypeStruct((FBL, TOK, BLK), BF16)
BUNDLE = jax.ShapeDtypeStruct((SIDE, TOK, WIDTH), BF16)
PIECE = jax.ShapeDtypeStruct((TOK, WIDTH), BF16)


def first_norm(micro, place, inputs, gain):
    return pl.pallas_call(
        first_norm_kernel,
        grid_spec=pltpu.PrefetchScalarGridSpec(
            num_scalar_prefetch=2,
            grid=(1,),
            in_specs=[
                pl.BlockSpec((1, TOK, BLOCKS * BLK), lambda i, micro, place: (micro[0], 0, 0)),
                pl.BlockSpec((BLOCKS, 1, BLK), lambda i, micro, place: (0, 0, 0)),
            ],
            out_specs=[
                pl.BlockSpec((BLOCKS, TOK, BLK), lambda i, micro, place: (0, 0, 0)),
                pl.BlockSpec((SIDE, TOK, WIDTH), lambda i, micro, place: (0, 0, 0)),
            ],
        ),
        out_shape=[NORMED, BUNDLE],
        cost_estimate=cost(1, 6 << 20),
        compiler_params=PARAMS,
        name="first_norm",
    )(micro, place, inputs, gain)


def anywhere():
    return pl.BlockSpec(memory_space=pl.ANY)


def first_in(place, meta, normed, cells):
    return pl.pallas_call(
        first_in_kernel,
        in_specs=[smem(), smem(), vmem()] + [anywhere()] * GRID_ROWS,
        out_specs=vmem(),
        out_shape=HIDDEN,
        scratch_shapes=[pltpu.VMEM((FBL + 1, TOK, BLK), F32)] + WORK,
        cost_estimate=cost(512, 8 << 20),
        compiler_params=PARAMS,
        name="first_in",
    )(place, meta, normed, *cells)


def later_in(place, meta, gain, bundles, cells):
    return pl.pallas_call(
        later_in_kernel,
        in_specs=[smem(), smem()] + [vmem()] * (1 + SIDE) + [anywhere()] * GRID_ROWS,
        out_specs=vmem(),
        out_shape=HIDDEN,
        scratch_shapes=[
            pltpu.VMEM((BLOCKS, TOK, BLK), BF16),
            pltpu.VMEM((FBL + 1, TOK, BLK), F32),
        ]
        + WORK,
        cost_estimate=cost(512, 12 << 20),
        compiler_params=PARAMS,
        name="later_in",
    )(place, meta, gain, *bundles, *cells)


def project_out(phase, place, meta, hidden, cells):
    return pl.pallas_call(
        functools.partial(out_kernel, phase),
        in_specs=[smem(), smem(), vmem()] + [anywhere()] * GRID_ROWS,
        out_specs=[vmem()] * SIDE,
        out_shape=[BUNDLE] * SIDE,
        scratch_shapes=[pltpu.VMEM((BLOCKS + 1, TOK, BLK), F32)] + WORK,
        cost_estimate=cost(512, 8 << 20),
        compiler_params=PARAMS,
        name="project_out",
    )(place, meta, hidden, *cells)


def add_up(kernel, place, bundles, outs):
    return pl.pallas_call(
        kernel,
        in_specs=([smem()] if place is not None else []) + [vmem()] * len(bundles),
        out_specs=[vmem()] * len(outs),
        out_shape=outs,
        cost_estimate=cost(0, 2 << 20),
        compiler_params=PARAMS,
    )(*([place] if place is not None else []), *bundles)


def on_rows(value, perm):
    return lax.ppermute(value, ("section", "row"), perm)


def on_cols(value, perm):
    return lax.ppermute(value, ("section", "col"), perm)


SWAP = [(i, (i + GRID_ROWS) % (2 * GRID_ROWS)) for i in range(2 * GRID_ROWS)]
AROUND = [(r, (r + 1) % GRID_ROWS) for r in range(GRID_ROWS)] + [
    (GRID_ROWS + r, GRID_ROWS + (r - 1) % GRID_ROWS) for r in range(GRID_ROWS)
]


DOWN = [(r, GRID_ROWS + (r - 1) % GRID_ROWS) for r in range(GRID_ROWS)]


def column_shift(first, distance):
    pairs = []
    for core in range(2):
        for y in range(SIDE):
            for x in range(SIDE):
                along_x = (core == 0) == first
                to_y = y if along_x else (y + distance) % SIDE
                to_x = (x + distance) % SIDE if along_x else x
                base = core * SIDE * SIDE
                pairs.append((base + y * SIDE + x, base + to_y * SIDE + to_x))
    return pairs


NEAR_GROUPS = [[y * SIDE + x for y in range(SIDE)] for x in range(SIDE)] + [
    [SIDE * SIDE + y * SIDE + x for x in range(SIDE)] for y in range(SIDE)
]


def ring_gather(cell, first=None):
    ring = [cell]
    other = []
    for step in range(1, GRID_ROWS // 2 + 1):
        if step == 1 and first is not None:
            ring.append(first)
        else:
            ring.append(on_rows(ring[-1], AROUND))
        if step < GRID_ROWS // 2:
            other.append(on_rows(ring[-1], SWAP))
    return ring + other


def first_step(mine, own):
    up = on_rows(own, AROUND[:GRID_ROWS])
    down = on_rows(own, DOWN)
    return jnp.where(mine, up, down)


def spread(values, first):
    landed = []
    for d in range(1, SIDE):
        value = values[d] if isinstance(values, (list, tuple)) else values
        landed.append(on_cols(value, column_shift(first, d)))
    return landed


def shards(inputs, norm_gain, w_in, w_in_slot, w_in_count, w_out, w_out_slot, w_out_count):
    core = lax.axis_index("section")
    row = lax.axis_index("row")
    col = lax.axis_index("col")
    y, x = col // SIDE, col % SIDE
    first = jnp.where(core == 0, x, y)
    second = jnp.where(core == 0, y, x)
    place = jnp.stack([core, col, first, second, row]).astype(jnp.int32)
    micro = jnp.reshape(core, (1,)).astype(jnp.int32)

    own_meta = jnp.concatenate(
        [
            w_in_slot.reshape(SLOTS),
            w_in_count.reshape(1),
            w_out_slot.reshape(SLOTS),
            w_out_count.reshape(1),
            jnp.zeros((BLK - 2 * SLOTS - 2,), jnp.int32),
        ]
    )
    meta = lax.all_to_all(
        jnp.broadcast_to(own_meta, (2 * GRID_ROWS, 1, BLK)),
        ("section", "row"),
        0,
        0,
        tiled=True,
    ).reshape(2 * GRID_ROWS, BLK)
    own_in = w_in.reshape(SLOTS * BLK, BLK)
    own_out = w_out.reshape(SLOTS * BLK, BLK)
    own_gain = norm_gain.reshape(BLOCKS, 1, BLK)
    other_in = on_rows(own_in, SWAP)
    other_out = on_rows(own_out, SWAP)
    other_gain = on_rows(own_gain, SWAP)
    mine = core == 0
    first_ins = first_step(mine, own_in)
    first_outs = first_step(mine, own_out)
    cells_in = ring_gather(jnp.where(mine, own_in, other_in), first_ins)
    cells_out = ring_gather(jnp.where(mine, own_out, other_out), first_outs)
    own_in, own_out, other_in, other_out, _ = lax.optimization_barrier(
        (own_in, own_out, other_in, other_out, cells_in[2])
    )
    later_cells = ring_gather(
        jnp.concatenate(
            [jnp.where(mine, other_in, own_in), jnp.where(mine, other_out, own_out)]
        ),
    )
    gains = [jnp.where(mine, own_gain, other_gain), jnp.where(mine, other_gain, own_gain)]

    normed, own_x = first_norm(micro, place, inputs, gains[0])
    hidden = first_in(place, meta, normed, cells_in)
    bundles = project_out(0, place, meta, hidden, cells_out)
    landed = spread(bundles, True)
    sums = add_up(whole_sum_kernel, None, [bundles[0]] + landed, [BUNDLE])[0]
    landed = spread(sums, False)
    middle, piece = add_up(merge_kernel, place, [own_x, sums] + landed, [BUNDLE, PIECE])

    bundles = [middle] + spread(middle, True)
    hidden = later_in(place, meta, gains[1], bundles, later_cells)
    bundles = project_out(1, place, meta, hidden, later_cells)
    landed = spread(bundles, True)
    sums = add_up(whole_sum_kernel, None, [bundles[0]] + landed, [BUNDLE])[0]
    landed = lax.all_to_all(
        sums, ("section", "col"), 0, 0, tiled=True, axis_index_groups=NEAR_GROUPS
    )
    final = (piece.astype(F32) + jnp.sum(landed.astype(F32), axis=0)).astype(BF16)

    other = on_rows(jnp.where(mine, final, piece), SWAP)
    return jnp.stack([jnp.where(mine, piece, other), jnp.where(mine, other, final)])[None]


def solution(mesh):
    placed = (
        P(None, "row", None),
        P("section", None),
        P("section", "row", "col", None, None, None),
        P("section", "row", "col", None),
        P("section", "row", "col"),
        P("section", "row", "col", None, None, None),
        P("section", "row", "col", None),
        P("section", "row", "col"),
    )

    return jax.shard_map(
        shards,
        mesh=mesh,
        in_specs=placed,
        out_specs=P("section", None, "row", "col"),
        check_vma=False,
    )
```

```python
import functools

import jax
import jax.numpy as jnp
from jax import lax
from jax.experimental import pallas as pl
from jax.experimental.pallas import tpu as pltpu
from jax.sharding import PartitionSpec as P


EPSILON = 1e-05
BLK = 128
SLOTS = 8
UNROLL = 4
TAIL = 16
SPAN = 1024 + TAIL
GRID_ROWS = 8
SIDE = 4
DBL = 6
FBL = 12
BLOCKS = 48
CHUNK = 3
TOK = 128
WIDTH = CHUNK * BLK


F32 = jnp.float32
BF16 = jnp.bfloat16


def vmem():
    return pl.BlockSpec(memory_space=pltpu.VMEM)


def smem():
    return pl.BlockSpec(memory_space=pltpu.SMEM)


def chunk_of(place_ref, first, second):
    core = place_ref[0]
    return jnp.where(core == 0, second * SIDE + first, first * SIDE + second)


def digit(value):
    return lax.rem(value + 2 * SIDE, SIDE)


def pack_kernel(place_ref, *refs):
    sources, outs, sems = refs[:6], refs[6:8], refs[8]
    copies = [
        pltpu.make_async_copy(sources[k], outs[k].at[pl.ds(0, SLOTS * BLK)], sems.at[k])
        for k in range(2)
    ]
    for copy in copies:
        copy.start()
    lane = lax.broadcasted_iota(jnp.int32, (TAIL, BLK), 1)
    for k, out in enumerate(outs):
        slots, count = sources[2 + k], sources[4 + k]
        row = jnp.where(lane == 2 * SLOTS, count[0], 0)
        for n in range(SLOTS):
            model, hid = place_ref[4] * DBL + slots[n] // FBL, lax.rem(slots[n], FBL)
            row = jnp.where(lane == n, hid if k else model, row)
            row = jnp.where(lane == SLOTS + n, model if k else hid, row)
        out[SLOTS * BLK : SPAN, :] = row.astype(F32).astype(BF16)
    for copy in copies:
        copy.wait()


def fetch(cells, offset, weights, tails, sems):
    size = SLOTS * BLK
    copies = []
    for i, cell in enumerate(cells):
        copies.append(
            pltpu.make_async_copy(
                cell.at[pl.ds(offset + size, TAIL)], tails.at[pl.ds(i * TAIL, TAIL)], sems.at[1, i]
            )
        )
    for i, cell in enumerate(cells):
        copies.append(
            pltpu.make_async_copy(
                cell.at[pl.ds(offset, size)], weights.at[pl.ds(i * size, size)], sems.at[0, i]
            )
        )
    for copy in copies:
        copy.start()
    return copies[:GRID_ROWS], copies[GRID_ROWS:]


def read_table(copies, tails, table):
    for copy in copies:
        copy.wait()
    for i in range(GRID_ROWS):
        rows = tails[i * TAIL : (i + 1) * TAIL, :].astype(F32).astype(jnp.int32)
        table[i : i + 1, :] = rows[0:1, :]


def list_blocks(table, small, dummy, blocks):
    pltpu.sync_copy(table, small)
    used = 0
    for i in range(GRID_ROWS):
        for n in range(SLOTS):
            blocks[0, used + n] = i * SLOTS + n
            blocks[1, used + n] = small[i, n]
            blocks[2, used + n] = small[i, SLOTS + n]
        used = used + small[i, 2 * SLOTS]
    for n in range(UNROLL):
        blocks[0, used + n] = 0
        blocks[1, used + n] = 0
        blocks[2, used + n] = dummy
    return used


def block_sum(dense, weights, blocks, used, total):
    def group(step, carry):
        at = step * UNROLL
        products = [
            jnp.dot(
                dense[blocks[1, at + u]],
                weights[pl.ds(pl.multiple_of(blocks[0, at + u] * BLK, BLK), BLK), :],
                preferred_element_type=F32,
            )
            for u in range(UNROLL)
        ]
        for u, product in enumerate(products):
            total[blocks[2, at + u]] += product
        return carry

    lax.fori_loop(0, (used + UNROLL - 1) // UNROLL, group, 0)


def gelu_into(total, hidden):
    for f in range(FBL):
        hidden[f] = jax.nn.gelu(total[f], approximate=True).astype(BF16)


def first_norm_kernel(micro_ref, place_ref, x_ref, gain_ref, normed_ref, own_ref):
    squares = jnp.zeros((TOK, BLK), F32)
    for k in range(BLOCKS):
        part = x_ref[0, :, k * BLK : (k + 1) * BLK].astype(F32)
        squares = squares + part * part
    mean = jnp.sum(squares, axis=1, keepdims=True) / (BLOCKS * BLK)
    scale = lax.rsqrt(mean + EPSILON)
    for k in range(BLOCKS):
        part = x_ref[0, :, k * BLK : (k + 1) * BLK].astype(F32)
        normed_ref[k] = (part * scale * gain_ref[k]).astype(BF16)
    for e in range(SIDE):
        start = pl.multiple_of(chunk_of(place_ref, place_ref[2], e) * WIDTH, BLK)
        own_ref[e] = x_ref[0, :, pl.ds(start, WIDTH)]


def first_in_kernel(normed_ref, *refs):
    cells = refs[:GRID_ROWS]
    hidden_ref, total, weights, tails, table, small, blocks, sems = refs[GRID_ROWS:]
    tail_copies, copies = fetch(cells, 0, weights, tails, sems)
    read_table(tail_copies, tails, table)
    total[...] = jnp.zeros_like(total)
    used = list_blocks(table, small, FBL, blocks)
    for copy in copies:
        copy.wait()
    block_sum(normed_ref, weights, blocks, used, total)
    gelu_into(total, hidden_ref)


def later_in_kernel(place_ref, gain_ref, *refs):
    bundles = refs[:SIDE]
    cells = refs[SIDE : SIDE + GRID_ROWS]
    hidden_ref, normed, total, weights, tails, table, small, blocks, sems = refs[SIDE + GRID_ROWS :]
    tail_copies, copies = fetch(cells, 0, weights, tails, sems)
    read_table(tail_copies, tails, table)
    squares = jnp.zeros((TOK, BLK), F32)
    for d in range(SIDE):
        for e in range(SIDE):
            for q in range(CHUNK):
                part = bundles[d][e, :, q * BLK : (q + 1) * BLK].astype(F32)
                squares = squares + part * part
    mean = jnp.sum(squares, axis=1, keepdims=True) / (BLOCKS * BLK)
    scale = lax.rsqrt(mean + EPSILON)
    for d in range(SIDE):
        for e in range(SIDE):
            chunk = chunk_of(place_ref, digit(place_ref[2] - d), e)
            for q in range(CHUNK):
                k = chunk * CHUNK + q
                part = bundles[d][e, :, q * BLK : (q + 1) * BLK].astype(F32)
                normed[k] = (part * scale * gain_ref[k]).astype(BF16)
    total[...] = jnp.zeros_like(total)
    used = list_blocks(table, small, FBL, blocks)
    for copy in copies:
        copy.wait()
    block_sum(normed, weights, blocks, used, total)
    gelu_into(total, hidden_ref)


def out_kernel(phase, place_ref, hidden_ref, *refs):
    cells = refs[:GRID_ROWS]
    sends = refs[GRID_ROWS : GRID_ROWS + SIDE]
    total, weights, tails, table, small, blocks, sems = refs[GRID_ROWS + SIDE :]
    tail_copies, copies = fetch(cells, phase * SPAN, weights, tails, sems)
    read_table(tail_copies, tails, table)
    total[...] = jnp.zeros_like(total)
    used = list_blocks(table, small, BLOCKS, blocks)
    for copy in copies:
        copy.wait()
    block_sum(hidden_ref, weights, blocks, used, total)
    for d in range(SIDE):
        for e in range(SIDE):
            second = digit(place_ref[3] + e) if phase else e
            chunk = chunk_of(place_ref, digit(place_ref[2] + d), second)
            for q in range(CHUNK):
                sends[d][e, :, q * BLK : (q + 1) * BLK] = total[chunk * CHUNK + q].astype(BF16)


def sum_of(refs, index):
    value = refs[0][index].astype(F32)
    for ref in refs[1:]:
        value = value + ref[index].astype(F32)
    return value


def whole_sum_kernel(*refs):
    for e in range(SIDE):
        refs[-1][e] = sum_of(refs[:-1], e).astype(BF16)


def merge_kernel(place_ref, *refs):
    bundle_ref, piece_ref = refs[-2:]
    for e in range(SIDE):
        bundle_ref[e] = sum_of(refs[:-2], e).astype(BF16)
    piece_ref[...] = bundle_ref[place_ref[3]]


def piece_sum_kernel(*refs):
    for e, piece in enumerate(refs[SIDE:]):
        piece[...] = sum_of(refs[:SIDE], e).astype(piece.dtype)


def cost(blocks, moved):
    return pl.CostEstimate(flops=blocks * 2 * BLK**3, bytes_accessed=moved, transcendentals=0)


WORK = [
    pltpu.VMEM((GRID_ROWS * SLOTS * BLK, BLK), BF16),
    pltpu.VMEM((GRID_ROWS * TAIL, BLK), BF16),
    pltpu.VMEM((GRID_ROWS, BLK), jnp.int32),
    pltpu.SMEM((GRID_ROWS, BLK), jnp.int32),
    pltpu.SMEM((3, GRID_ROWS * SLOTS + 2 * SLOTS), jnp.int32),
    pltpu.SemaphoreType.DMA((2, GRID_ROWS)),
]
PARAMS = pltpu.CompilerParams(vmem_limit_bytes=16 << 20)
NORMED = jax.ShapeDtypeStruct((BLOCKS, TOK, BLK), BF16)
HIDDEN = jax.ShapeDtypeStruct((FBL, TOK, BLK), BF16)
BUNDLE = jax.ShapeDtypeStruct((SIDE, TOK, WIDTH), BF16)
PIECE = jax.ShapeDtypeStruct((TOK, WIDTH), BF16)


def first_norm(micro, place, inputs, gain):
    return pl.pallas_call(
        first_norm_kernel,
        grid_spec=pltpu.PrefetchScalarGridSpec(
            num_scalar_prefetch=2,
            grid=(1,),
            in_specs=[
                pl.BlockSpec((1, TOK, BLOCKS * BLK), lambda i, micro, place: (micro[0], 0, 0)),
                pl.BlockSpec((BLOCKS, 1, BLK), lambda i, micro, place: (0, 0, 0)),
            ],
            out_specs=[
                pl.BlockSpec((BLOCKS, TOK, BLK), lambda i, micro, place: (0, 0, 0)),
                pl.BlockSpec((SIDE, TOK, WIDTH), lambda i, micro, place: (0, 0, 0)),
            ],
        ),
        out_shape=[NORMED, BUNDLE],
        cost_estimate=cost(1, 6 << 20),
        compiler_params=PARAMS,
        name="first_norm",
    )(micro, place, inputs, gain)


def anywhere():
    return pl.BlockSpec(memory_space=pl.ANY)


def first_in(normed, cells):
    return pl.pallas_call(
        first_in_kernel,
        in_specs=[vmem()] + [anywhere()] * GRID_ROWS,
        out_specs=vmem(),
        out_shape=HIDDEN,
        scratch_shapes=[pltpu.VMEM((FBL + 1, TOK, BLK), F32)] + WORK,
        cost_estimate=cost(512, 8 << 20),
        compiler_params=PARAMS,
        name="first_in",
    )(normed, *cells)


def later_in(place, gain, bundles, cells):
    return pl.pallas_call(
        later_in_kernel,
        in_specs=[smem()] + [vmem()] * (1 + SIDE) + [anywhere()] * GRID_ROWS,
        out_specs=vmem(),
        out_shape=HIDDEN,
        scratch_shapes=[
            pltpu.VMEM((BLOCKS, TOK, BLK), BF16),
            pltpu.VMEM((FBL + 1, TOK, BLK), F32),
        ]
        + WORK,
        cost_estimate=cost(512, 12 << 20),
        compiler_params=PARAMS,
        name="later_in",
    )(place, gain, *bundles, *cells)


def project_out(phase, place, hidden, cells):
    return pl.pallas_call(
        functools.partial(out_kernel, phase),
        in_specs=[smem(), vmem()] + [anywhere()] * GRID_ROWS,
        out_specs=[vmem()] * SIDE,
        out_shape=[BUNDLE] * SIDE,
        scratch_shapes=[pltpu.VMEM((BLOCKS + 1, TOK, BLK), F32)] + WORK,
        cost_estimate=cost(512, 8 << 20),
        compiler_params=PARAMS,
        name="project_out",
    )(place, hidden, *cells)


def pack(place, *sources):
    shape = jax.ShapeDtypeStruct((SPAN, BLK), BF16)
    return pl.pallas_call(
        pack_kernel,
        in_specs=[smem()] + [anywhere()] * 2 + [smem()] * 4,
        out_specs=[vmem()] * 2,
        out_shape=[shape] * 2,
        scratch_shapes=[pltpu.SemaphoreType.DMA((2,))],
        cost_estimate=cost(0, 1 << 20),
        compiler_params=PARAMS,
        name="pack",
    )(place, *sources)


def add_up(kernel, place, bundles, outs):
    return pl.pallas_call(
        kernel,
        in_specs=([smem()] if place is not None else []) + [vmem()] * len(bundles),
        out_specs=[vmem()] * len(outs),
        out_shape=outs,
        cost_estimate=cost(0, 2 << 20),
        compiler_params=PARAMS,
    )(*([place] if place is not None else []), *bundles)


def on_rows(value, perm):
    return lax.ppermute(value, ("section", "row"), perm)


def on_cols(value, perm):
    return lax.ppermute(value, ("section", "col"), perm)


SWAP = [(i, (i + GRID_ROWS) % (2 * GRID_ROWS)) for i in range(2 * GRID_ROWS)]
AROUND = [(r, (r + 1) % GRID_ROWS) for r in range(GRID_ROWS)] + [
    (GRID_ROWS + r, GRID_ROWS + (r - 1) % GRID_ROWS) for r in range(GRID_ROWS)
]


def column_shift(first, distance):
    pairs = []
    for core in range(2):
        for y in range(SIDE):
            for x in range(SIDE):
                along_x = (core == 0) == first
                to_y = y if along_x else (y + distance) % SIDE
                to_x = (x + distance) % SIDE if along_x else x
                base = core * SIDE * SIDE
                pairs.append((base + y * SIDE + x, base + to_y * SIDE + to_x))
    return pairs


def ring_gather(cell):
    ring = [cell]
    other = []
    for step in range(1, GRID_ROWS // 2 + 1):
        ring.append(on_rows(ring[-1], AROUND))
        if step < GRID_ROWS // 2:
            other.append(on_rows(ring[-1], SWAP))
    return ring + other


def spread(values, first):
    landed = []
    for d in range(1, SIDE):
        value = values[d] if isinstance(values, (list, tuple)) else values
        landed.append(on_cols(value, column_shift(first, d)))
    return landed


def shards(inputs, norm_gain, w_in, w_in_slot, w_in_count, w_out, w_out_slot, w_out_count):
    core = lax.axis_index("section")
    row = lax.axis_index("row")
    col = lax.axis_index("col")
    y, x = col // SIDE, col % SIDE
    first = jnp.where(core == 0, x, y)
    second = jnp.where(core == 0, y, x)
    place = jnp.stack([core, col, first, second, row]).astype(jnp.int32)
    micro = jnp.reshape(core, (1,)).astype(jnp.int32)

    own_in, own_out = pack(
        place,
        w_in.reshape(SLOTS * BLK, BLK),
        w_out.reshape(SLOTS * BLK, BLK),
        w_in_slot.reshape(SLOTS),
        w_out_slot.reshape(SLOTS),
        w_in_count.reshape(1),
        w_out_count.reshape(1),
    )
    own_gain = norm_gain.reshape(BLOCKS, 1, BLK)
    other_in = on_rows(own_in, SWAP)
    other_out = on_rows(own_out, SWAP)
    other_gain = on_rows(own_gain, SWAP)
    mine = core == 0
    cells_in = ring_gather(jnp.where(mine, own_in, other_in))
    cells_out = ring_gather(jnp.where(mine, own_out, other_out))
    own_in, own_out, other_in, other_out, _ = lax.optimization_barrier(
        (own_in, own_out, other_in, other_out, cells_in[2])
    )
    later_cells = ring_gather(
        jnp.concatenate(
            [jnp.where(mine, other_in, own_in), jnp.where(mine, other_out, own_out)]
        ),
    )
    gains = [jnp.where(mine, own_gain, other_gain), jnp.where(mine, other_gain, own_gain)]

    normed, own_x = first_norm(micro, place, inputs, gains[0])
    hidden = first_in(normed, cells_in)
    bundles = project_out(0, place, hidden, cells_out)
    landed = spread(bundles, True)
    sums = add_up(whole_sum_kernel, None, [bundles[0]] + landed, [BUNDLE])[0]
    landed = spread(sums, False)
    middle, piece = add_up(merge_kernel, place, [own_x, sums] + landed, [BUNDLE, PIECE])

    bundles = [middle] + spread(middle, True)
    hidden = later_in(place, gains[1], bundles, later_cells)
    bundles = project_out(1, place, hidden, later_cells)
    landed = spread(bundles, True)
    sums = add_up(
        piece_sum_kernel,
        None,
        [bundles[0]] + landed,
        [jax.ShapeDtypeStruct((TOK, WIDTH), F32)] + [PIECE] * (SIDE - 1),
    )
    total = sums[0]
    for value in spread(sums, False):
        total = total + value.astype(F32)
    final = (piece.astype(F32) + total).astype(BF16)

    other = on_rows(jnp.where(mine, final, piece), SWAP)
    return jnp.stack([jnp.where(mine, piece, other), jnp.where(mine, other, final)])[None]


def solution(mesh):
    placed = (
        P(None, "row", None),
        P("section", None),
        P("section", "row", "col", None, None, None),
        P("section", "row", "col", None),
        P("section", "row", "col"),
        P("section", "row", "col", None, None, None),
        P("section", "row", "col", None),
        P("section", "row", "col"),
    )

    return jax.shard_map(
        shards,
        mesh=mesh,
        in_specs=placed,
        out_specs=P("section", None, "row", "col"),
        check_vma=False,
    )
```

```python
import functools

import jax
import jax.numpy as jnp
from jax import lax
from jax.experimental import pallas as pl
from jax.experimental.pallas import tpu as pltpu
from jax.sharding import PartitionSpec as P


EPSILON = 1e-05
BLK = 128
SLOTS = 8
UNROLL = 4
TAIL = 16
SPAN = 1024 + TAIL
GRID_ROWS = 8
SIDE = 4
DBL = 6
FBL = 12
BLOCKS = 48
CHUNK = 3
TOK = 128
WIDTH = CHUNK * BLK


F32 = jnp.float32
BF16 = jnp.bfloat16


def vmem():
    return pl.BlockSpec(memory_space=pltpu.VMEM)


def smem():
    return pl.BlockSpec(memory_space=pltpu.SMEM)


def chunk_of(place_ref, first, second):
    core = place_ref[0]
    return jnp.where(core == 0, second * SIDE + first, first * SIDE + second)


def digit(value):
    return lax.rem(value + 2 * SIDE, SIDE)


def pack_kernel(place_ref, *refs):
    sources, outs, slots, counts, sems = refs[:6], refs[6:8], refs[8:10], refs[10:12], refs[12]
    small = [
        pltpu.make_async_copy(source, target, sems.at[2 + k])
        for k, (source, target) in enumerate(zip(sources[2:], slots + counts))
    ]
    copies = [
        pltpu.make_async_copy(sources[k], outs[k].at[pl.ds(0, SLOTS * BLK)], sems.at[k])
        for k in range(2)
    ]
    for copy in small + copies:
        copy.start()
    for copy in small:
        copy.wait()
    lane = lax.broadcasted_iota(jnp.int32, (TAIL, BLK), 1)
    for k, out in enumerate(outs):
        row = jnp.where(lane == 2 * SLOTS, counts[k][0], 0)
        for n in range(SLOTS):
            slot = slots[k][n]
            model, hid = place_ref[4] * DBL + slot // FBL, lax.rem(slot, FBL)
            row = jnp.where(lane == n, hid if k else model, row)
            row = jnp.where(lane == SLOTS + n, model if k else hid, row)
        out[SLOTS * BLK : SPAN, :] = row.astype(F32).astype(BF16)
    for copy in copies:
        copy.wait()


def fetch(cells, offset, weights, tails, sems):
    size = SLOTS * BLK
    copies = []
    for i, cell in enumerate(cells):
        copies.append(
            pltpu.make_async_copy(
                cell.at[pl.ds(offset + size, TAIL)], tails.at[pl.ds(i * TAIL, TAIL)], sems.at[1, i]
            )
        )
    for i, cell in enumerate(cells):
        copies.append(
            pltpu.make_async_copy(
                cell.at[pl.ds(offset, size)], weights.at[pl.ds(i * size, size)], sems.at[0, i]
            )
        )
    for copy in copies:
        copy.start()
    return copies[:GRID_ROWS], copies[GRID_ROWS:]


def read_table(copies, tails, table):
    for copy in copies:
        copy.wait()
    for i in range(GRID_ROWS):
        rows = tails[i * TAIL : (i + 1) * TAIL, :].astype(F32).astype(jnp.int32)
        table[i : i + 1, :] = rows[0:1, :]


def list_blocks(table, small, dummy, blocks):
    pltpu.sync_copy(table, small)
    used = 0
    for i in range(GRID_ROWS):
        for n in range(SLOTS):
            blocks[0, used + n] = i * SLOTS + n
            blocks[1, used + n] = small[i, n]
            blocks[2, used + n] = small[i, SLOTS + n]
        used = used + small[i, 2 * SLOTS]
    for n in range(UNROLL):
        blocks[0, used + n] = 0
        blocks[1, used + n] = 0
        blocks[2, used + n] = dummy
    return used


def block_sum(dense, weights, blocks, used, total):
    def group(step, carry):
        at = step * UNROLL
        products = [
            jnp.dot(
                dense[blocks[1, at + u]],
                weights[pl.ds(pl.multiple_of(blocks[0, at + u] * BLK, BLK), BLK), :],
                preferred_element_type=F32,
            )
            for u in range(UNROLL)
        ]
        for u, product in enumerate(products):
            total[blocks[2, at + u]] += product
        return carry

    lax.fori_loop(0, (used + UNROLL - 1) // UNROLL, group, 0)


def gelu_into(total, hidden):
    for f in range(FBL):
        hidden[f] = jax.nn.gelu(total[f], approximate=True).astype(BF16)


def first_norm_kernel(micro_ref, place_ref, x_ref, gain_ref, normed_ref, own_ref):
    squares = jnp.zeros((TOK, BLK), F32)
    for k in range(BLOCKS):
        part = x_ref[0, :, k * BLK : (k + 1) * BLK].astype(F32)
        squares = squares + part * part
    mean = jnp.sum(squares, axis=1, keepdims=True) / (BLOCKS * BLK)
    scale = lax.rsqrt(mean + EPSILON)
    for k in range(BLOCKS):
        part = x_ref[0, :, k * BLK : (k + 1) * BLK].astype(F32)
        normed_ref[k] = (part * scale * gain_ref[k]).astype(BF16)
    for e in range(SIDE):
        start = pl.multiple_of(chunk_of(place_ref, place_ref[2], e) * WIDTH, BLK)
        own_ref[e] = x_ref[0, :, pl.ds(start, WIDTH)]


def first_in_kernel(normed_ref, *refs):
    cells = refs[:GRID_ROWS]
    hidden_ref, total, weights, tails, table, small, blocks, sems = refs[GRID_ROWS:]
    tail_copies, copies = fetch(cells, 0, weights, tails, sems)
    read_table(tail_copies, tails, table)
    total[...] = jnp.zeros_like(total)
    used = list_blocks(table, small, FBL, blocks)
    for copy in copies:
        copy.wait()
    block_sum(normed_ref, weights, blocks, used, total)
    gelu_into(total, hidden_ref)


def later_in_kernel(place_ref, gain_ref, *refs):
    bundles = refs[:SIDE]
    cells = refs[SIDE : SIDE + GRID_ROWS]
    hidden_ref, normed, total, weights, tails, table, small, blocks, sems = refs[SIDE + GRID_ROWS :]
    tail_copies, copies = fetch(cells, 0, weights, tails, sems)
    read_table(tail_copies, tails, table)
    squares = jnp.zeros((TOK, BLK), F32)
    for d in range(SIDE):
        for e in range(SIDE):
            for q in range(CHUNK):
                part = bundles[d][e, :, q * BLK : (q + 1) * BLK].astype(F32)
                squares = squares + part * part
    mean = jnp.sum(squares, axis=1, keepdims=True) / (BLOCKS * BLK)
    scale = lax.rsqrt(mean + EPSILON)
    for d in range(SIDE):
        for e in range(SIDE):
            chunk = chunk_of(place_ref, digit(place_ref[2] - d), e)
            for q in range(CHUNK):
                k = chunk * CHUNK + q
                part = bundles[d][e, :, q * BLK : (q + 1) * BLK].astype(F32)
                normed[k] = (part * scale * gain_ref[k]).astype(BF16)
    total[...] = jnp.zeros_like(total)
    used = list_blocks(table, small, FBL, blocks)
    for copy in copies:
        copy.wait()
    block_sum(normed, weights, blocks, used, total)
    gelu_into(total, hidden_ref)


def out_kernel(phase, place_ref, hidden_ref, *refs):
    cells = refs[:GRID_ROWS]
    sends = refs[GRID_ROWS : GRID_ROWS + SIDE]
    total, weights, tails, table, small, blocks, sems = refs[GRID_ROWS + SIDE :]
    tail_copies, copies = fetch(cells, phase * SPAN, weights, tails, sems)
    read_table(tail_copies, tails, table)
    total[...] = jnp.zeros_like(total)
    used = list_blocks(table, small, BLOCKS, blocks)
    for copy in copies:
        copy.wait()
    block_sum(hidden_ref, weights, blocks, used, total)
    for d in range(SIDE):
        for e in range(SIDE):
            second = digit(place_ref[3] + e) if phase else e
            chunk = chunk_of(place_ref, digit(place_ref[2] + d), second)
            for q in range(CHUNK):
                sends[d][e, :, q * BLK : (q + 1) * BLK] = total[chunk * CHUNK + q].astype(BF16)


def sum_of(refs, index):
    value = refs[0][index].astype(F32)
    for ref in refs[1:]:
        value = value + ref[index].astype(F32)
    return value


def whole_sum_kernel(*refs):
    for e in range(SIDE):
        refs[-1][e] = sum_of(refs[:-1], e).astype(BF16)


def merge_kernel(place_ref, *refs):
    bundle_ref, piece_ref = refs[-2:]
    for e in range(SIDE):
        bundle_ref[e] = sum_of(refs[:-2], e).astype(BF16)
    piece_ref[...] = bundle_ref[place_ref[3]]


def piece_sum_kernel(*refs):
    for e, piece in enumerate(refs[SIDE:]):
        piece[...] = sum_of(refs[:SIDE], e).astype(piece.dtype)


def cost(blocks, moved):
    return pl.CostEstimate(flops=blocks * 2 * BLK**3, bytes_accessed=moved, transcendentals=0)


WORK = [
    pltpu.VMEM((GRID_ROWS * SLOTS * BLK, BLK), BF16),
    pltpu.VMEM((GRID_ROWS * TAIL, BLK), BF16),
    pltpu.VMEM((GRID_ROWS, BLK), jnp.int32),
    pltpu.SMEM((GRID_ROWS, BLK), jnp.int32),
    pltpu.SMEM((3, GRID_ROWS * SLOTS + 2 * SLOTS), jnp.int32),
    pltpu.SemaphoreType.DMA((2, GRID_ROWS)),
]
PARAMS = pltpu.CompilerParams(vmem_limit_bytes=16 << 20)
NORMED = jax.ShapeDtypeStruct((BLOCKS, TOK, BLK), BF16)
HIDDEN = jax.ShapeDtypeStruct((FBL, TOK, BLK), BF16)
BUNDLE = jax.ShapeDtypeStruct((SIDE, TOK, WIDTH), BF16)
PIECE = jax.ShapeDtypeStruct((TOK, WIDTH), BF16)


def first_norm(micro, place, inputs, gain):
    return pl.pallas_call(
        first_norm_kernel,
        grid_spec=pltpu.PrefetchScalarGridSpec(
            num_scalar_prefetch=2,
            grid=(1,),
            in_specs=[
                pl.BlockSpec((1, TOK, BLOCKS * BLK), lambda i, micro, place: (micro[0], 0, 0)),
                pl.BlockSpec((BLOCKS, 1, BLK), lambda i, micro, place: (0, 0, 0)),
            ],
            out_specs=[
                pl.BlockSpec((BLOCKS, TOK, BLK), lambda i, micro, place: (0, 0, 0)),
                pl.BlockSpec((SIDE, TOK, WIDTH), lambda i, micro, place: (0, 0, 0)),
            ],
        ),
        out_shape=[NORMED, BUNDLE],
        cost_estimate=cost(1, 6 << 20),
        compiler_params=PARAMS,
        name="first_norm",
    )(micro, place, inputs, gain)


def anywhere():
    return pl.BlockSpec(memory_space=pl.ANY)


def first_in(normed, cells):
    return pl.pallas_call(
        first_in_kernel,
        in_specs=[vmem()] + [anywhere()] * GRID_ROWS,
        out_specs=vmem(),
        out_shape=HIDDEN,
        scratch_shapes=[pltpu.VMEM((FBL + 1, TOK, BLK), F32)] + WORK,
        cost_estimate=cost(512, 8 << 20),
        compiler_params=PARAMS,
        name="first_in",
    )(normed, *cells)


def later_in(place, gain, bundles, cells):
    return pl.pallas_call(
        later_in_kernel,
        in_specs=[smem()] + [vmem()] * (1 + SIDE) + [anywhere()] * GRID_ROWS,
        out_specs=vmem(),
        out_shape=HIDDEN,
        scratch_shapes=[
            pltpu.VMEM((BLOCKS, TOK, BLK), BF16),
            pltpu.VMEM((FBL + 1, TOK, BLK), F32),
        ]
        + WORK,
        cost_estimate=cost(512, 12 << 20),
        compiler_params=PARAMS,
        name="later_in",
    )(place, gain, *bundles, *cells)


def project_out(phase, place, hidden, cells):
    return pl.pallas_call(
        functools.partial(out_kernel, phase),
        in_specs=[smem(), vmem()] + [anywhere()] * GRID_ROWS,
        out_specs=[vmem()] * SIDE,
        out_shape=[BUNDLE] * SIDE,
        scratch_shapes=[pltpu.VMEM((BLOCKS + 1, TOK, BLK), F32)] + WORK,
        cost_estimate=cost(512, 8 << 20),
        compiler_params=PARAMS,
        name="project_out",
    )(place, hidden, *cells)


def pack(place, *sources):
    shape = jax.ShapeDtypeStruct((SPAN, BLK), BF16)
    return pl.pallas_call(
        pack_kernel,
        in_specs=[smem()] + [pl.BlockSpec(memory_space=pltpu.HBM)] * 6,
        out_specs=[vmem()] * 2,
        out_shape=[shape] * 2,
        scratch_shapes=[pltpu.SMEM((SLOTS,), jnp.int32)] * 2
        + [pltpu.SMEM((1,), jnp.int32)] * 2
        + [pltpu.SemaphoreType.DMA((6,))],
        cost_estimate=cost(0, 1 << 20),
        compiler_params=PARAMS,
        name="pack",
    )(place, *[pltpu.with_memory_space_constraint(v, pltpu.HBM) for v in sources[:4]], *sources[4:])


def add_up(kernel, place, bundles, outs):
    return pl.pallas_call(
        kernel,
        in_specs=([smem()] if place is not None else []) + [vmem()] * len(bundles),
        out_specs=[vmem()] * len(outs),
        out_shape=outs,
        cost_estimate=cost(0, 2 << 20),
        compiler_params=PARAMS,
    )(*([place] if place is not None else []), *bundles)


def on_rows(value, perm):
    return lax.ppermute(value, ("section", "row"), perm)


def on_cols(value, perm):
    return lax.ppermute(value, ("section", "col"), perm)


SWAP = [(i, (i + GRID_ROWS) % (2 * GRID_ROWS)) for i in range(2 * GRID_ROWS)]
AROUND = [(r, (r + 1) % GRID_ROWS) for r in range(GRID_ROWS)] + [
    (GRID_ROWS + r, GRID_ROWS + (r - 1) % GRID_ROWS) for r in range(GRID_ROWS)
]


def column_shift(first, distance):
    pairs = []
    for core in range(2):
        for y in range(SIDE):
            for x in range(SIDE):
                along_x = (core == 0) == first
                to_y = y if along_x else (y + distance) % SIDE
                to_x = (x + distance) % SIDE if along_x else x
                base = core * SIDE * SIDE
                pairs.append((base + y * SIDE + x, base + to_y * SIDE + to_x))
    return pairs


def ring_gather(cell):
    ring = [cell]
    other = []
    for step in range(1, GRID_ROWS // 2 + 1):
        ring.append(on_rows(ring[-1], AROUND))
        if step < GRID_ROWS // 2:
            other.append(on_rows(ring[-1], SWAP))
    return ring + other


def spread(values, first):
    landed = []
    for d in range(1, SIDE):
        value = values[d] if isinstance(values, (list, tuple)) else values
        landed.append(on_cols(value, column_shift(first, d)))
    return landed


def shards(inputs, norm_gain, w_in, w_in_slot, w_in_count, w_out, w_out_slot, w_out_count):
    core = lax.axis_index("section")
    row = lax.axis_index("row")
    col = lax.axis_index("col")
    y, x = col // SIDE, col % SIDE
    first = jnp.where(core == 0, x, y)
    second = jnp.where(core == 0, y, x)
    place = jnp.stack([core, col, first, second, row]).astype(jnp.int32)
    micro = jnp.reshape(core, (1,)).astype(jnp.int32)

    own_in, own_out = pack(
        place,
        w_in.reshape(SLOTS * BLK, BLK),
        w_out.reshape(SLOTS * BLK, BLK),
        w_in_slot.reshape(SLOTS),
        w_out_slot.reshape(SLOTS),
        w_in_count.reshape(1),
        w_out_count.reshape(1),
    )
    own_gain = norm_gain.reshape(BLOCKS, 1, BLK)
    other_in = on_rows(own_in, SWAP)
    other_out = on_rows(own_out, SWAP)
    other_gain = on_rows(own_gain, SWAP)
    mine = core == 0
    cells_in = ring_gather(jnp.where(mine, own_in, other_in))
    cells_out = ring_gather(jnp.where(mine, own_out, other_out))
    own_in, own_out, other_in, other_out, _ = lax.optimization_barrier(
        (own_in, own_out, other_in, other_out, cells_in[2])
    )
    later_cells = ring_gather(
        jnp.concatenate(
            [jnp.where(mine, other_in, own_in), jnp.where(mine, other_out, own_out)]
        ),
    )
    gains = [jnp.where(mine, own_gain, other_gain), jnp.where(mine, other_gain, own_gain)]

    normed, own_x = first_norm(micro, place, inputs, gains[0])
    hidden = first_in(normed, cells_in)
    bundles = project_out(0, place, hidden, cells_out)
    landed = spread(bundles, True)
    sums = add_up(whole_sum_kernel, None, [bundles[0]] + landed, [BUNDLE])[0]
    landed = spread(sums, False)
    middle, piece = add_up(merge_kernel, place, [own_x, sums] + landed, [BUNDLE, PIECE])

    bundles = [middle] + spread(middle, True)
    hidden = later_in(place, gains[1], bundles, later_cells)
    bundles = project_out(1, place, hidden, later_cells)
    landed = spread(bundles, True)
    sums = add_up(
        piece_sum_kernel,
        None,
        [bundles[0]] + landed,
        [jax.ShapeDtypeStruct((TOK, WIDTH), F32)] + [PIECE] * (SIDE - 1),
    )
    total = sums[0]
    for value in spread(sums, False):
        total = total + value.astype(F32)
    final = (piece.astype(F32) + total).astype(BF16)

    other = on_rows(jnp.where(mine, final, piece), SWAP)
    return jnp.stack([jnp.where(mine, piece, other), jnp.where(mine, other, final)])[None]


def solution(mesh):
    placed = (
        P(None, "row", None),
        P("section", None),
        P("section", "row", "col", None, None, None),
        P("section", "row", "col", None),
        P("section", "row", "col"),
        P("section", "row", "col", None, None, None),
        P("section", "row", "col", None),
        P("section", "row", "col"),
    )

    return jax.shard_map(
        shards,
        mesh=mesh,
        in_specs=placed,
        out_specs=P("section", None, "row", "col"),
        check_vma=False,
    )
```

```python
import jax
import jax.numpy as jnp
from jax import lax
from jax.experimental import pallas as pl
from jax.experimental.pallas import tpu as pltpu
from jax.sharding import PartitionSpec as P


EPSILON = 1e-05
BLK = 128
SLOTS = 8
UNROLL = 4
TAIL = 16
SPAN = 1024 + TAIL
GRID_ROWS = 8
EARLY = (0, 1, 2, 3, 5, 6)
LATE = (4, 7)
SIDE = 4
DBL = 6
FBL = 12
BLOCKS = 48
CHUNK = 3
TOK = 128
WIDTH = CHUNK * BLK


F32 = jnp.float32
BF16 = jnp.bfloat16


def vmem():
    return pl.BlockSpec(memory_space=pltpu.VMEM)


def smem():
    return pl.BlockSpec(memory_space=pltpu.SMEM)


def chunk_of(place_ref, first, second):
    core = place_ref[0]
    return jnp.where(core == 0, second * SIDE + first, first * SIDE + second)


def digit(value):
    return lax.rem(value + 2 * SIDE, SIDE)


def pack_kernel(place_ref, *refs):
    sources, outs, slots, counts, sems = refs[:6], refs[6:8], refs[8:10], refs[10:12], refs[12]
    small = [
        pltpu.make_async_copy(source, target, sems.at[2 + k])
        for k, (source, target) in enumerate(zip(sources[2:], slots + counts))
    ]
    copies = [
        pltpu.make_async_copy(sources[k], outs[k].at[pl.ds(0, SLOTS * BLK)], sems.at[k])
        for k in range(2)
    ]
    for copy in small + copies:
        copy.start()
    for copy in small:
        copy.wait()
    lane = lax.broadcasted_iota(jnp.int32, (TAIL, BLK), 1)
    for k, out in enumerate(outs):
        row = jnp.where(lane == 2 * SLOTS, counts[k][0], 0)
        for n in range(SLOTS):
            slot = slots[k][n]
            model, hid = place_ref[4] * DBL + slot // FBL, lax.rem(slot, FBL)
            row = jnp.where(lane == n, hid if k else model, row)
            row = jnp.where(lane == SLOTS + n, model if k else hid, row)
        out[SLOTS * BLK : SPAN, :] = row.astype(F32).astype(BF16)
    for copy in copies:
        copy.wait()


def fetch(cells, offset, weights, tails, sems):
    size = SLOTS * BLK
    copies = []
    for i, cell in enumerate(cells):
        copies.append(
            pltpu.make_async_copy(
                cell.at[pl.ds(offset + size, TAIL)], tails.at[pl.ds(i * TAIL, TAIL)], sems.at[1, i]
            )
        )
    for i, cell in enumerate(cells):
        copies.append(
            pltpu.make_async_copy(
                cell.at[pl.ds(offset, size)], weights.at[pl.ds(i * size, size)], sems.at[0, i]
            )
        )
    for copy in copies:
        copy.start()
    return copies[: len(cells)], copies[len(cells) :]


def read_table(copies, tails, table):
    for copy in copies:
        copy.wait()
    for i in range(len(copies)):
        rows = tails[i * TAIL : (i + 1) * TAIL, :].astype(F32).astype(jnp.int32)
        table[i : i + 1, :] = rows[0:1, :]


def list_blocks(table, small, dummy, blocks):
    pltpu.sync_copy(table, small)
    used = 0
    for i in range(table.shape[0]):
        for n in range(SLOTS):
            blocks[0, used + n] = i * SLOTS + n
            blocks[1, used + n] = small[i, n]
            blocks[2, used + n] = small[i, SLOTS + n]
        used = used + small[i, 2 * SLOTS]
    for n in range(UNROLL):
        blocks[0, used + n] = 0
        blocks[1, used + n] = 0
        blocks[2, used + n] = dummy
    return used


def block_sum(dense, weights, blocks, used, total):
    def group(step, carry):
        at = step * UNROLL
        products = [
            jnp.dot(
                dense[blocks[1, at + u]],
                weights[pl.ds(pl.multiple_of(blocks[0, at + u] * BLK, BLK), BLK), :],
                preferred_element_type=F32,
            )
            for u in range(UNROLL)
        ]
        for u, product in enumerate(products):
            total[blocks[2, at + u]] += product
        return carry

    lax.fori_loop(0, (used + UNROLL - 1) // UNROLL, group, 0)


def gelu_into(total, hidden):
    for f in range(FBL):
        hidden[f] = jax.nn.gelu(total[f], approximate=True).astype(BF16)


def first_norm_kernel(micro_ref, place_ref, x_ref, gain_ref, normed_ref, own_ref):
    squares = jnp.zeros((TOK, BLK), F32)
    for k in range(BLOCKS):
        part = x_ref[0, :, k * BLK : (k + 1) * BLK].astype(F32)
        squares = squares + part * part
    mean = jnp.sum(squares, axis=1, keepdims=True) / (BLOCKS * BLK)
    scale = lax.rsqrt(mean + EPSILON)
    for k in range(BLOCKS):
        part = x_ref[0, :, k * BLK : (k + 1) * BLK].astype(F32)
        normed_ref[k] = (part * scale * gain_ref[k]).astype(BF16)
    for e in range(SIDE):
        start = pl.multiple_of(chunk_of(place_ref, place_ref[2], e) * WIDTH, BLK)
        own_ref[e] = x_ref[0, :, pl.ds(start, WIDTH)]


def early_in_kernel(normed_ref, *refs):
    cells = refs[: len(EARLY)]
    total, weights, tails, table, small, blocks, sems = refs[len(EARLY) :]
    tail_copies, copies = fetch(cells, 0, weights, tails, sems)
    read_table(tail_copies, tails, table)
    total[...] = jnp.zeros_like(total)
    used = list_blocks(table, small, FBL, blocks)
    for copy in copies:
        copy.wait()
    block_sum(normed_ref, weights, blocks, used, total)


def late_in_kernel(normed_ref, early_ref, *refs):
    cells = refs[: len(LATE)]
    hidden_ref, total, weights, tails, table, small, blocks, sems = refs[len(LATE) :]
    tail_copies, copies = fetch(cells, 0, weights, tails, sems)
    read_table(tail_copies, tails, table)
    total[...] = early_ref[...]
    used = list_blocks(table, small, FBL, blocks)
    for copy in copies:
        copy.wait()
    block_sum(normed_ref, weights, blocks, used, total)
    gelu_into(total, hidden_ref)


def send_out(place_ref, total, sends, relative):
    for d in range(SIDE):
        for e in range(SIDE):
            second = digit(place_ref[3] + e) if relative else e
            chunk = chunk_of(place_ref, digit(place_ref[2] + d), second)
            for q in range(CHUNK):
                sends[d][e, :, q * BLK : (q + 1) * BLK] = total[chunk * CHUNK + q].astype(BF16)


def early_out_kernel(hidden_ref, *refs):
    cells = refs[: len(EARLY)]
    total, weights, tails, table, small, blocks, sems = refs[len(EARLY) :]
    tail_copies, copies = fetch(cells, 0, weights, tails, sems)
    read_table(tail_copies, tails, table)
    total[...] = jnp.zeros_like(total)
    used = list_blocks(table, small, BLOCKS, blocks)
    for copy in copies:
        copy.wait()
    block_sum(hidden_ref, weights, blocks, used, total)


def late_out_kernel(place_ref, hidden_ref, early_ref, *refs):
    cells = refs[: len(LATE)]
    sends = refs[len(LATE) : len(LATE) + SIDE]
    total, weights, tails, table, small, blocks, sems = refs[len(LATE) + SIDE :]
    tail_copies, copies = fetch(cells, 0, weights, tails, sems)
    read_table(tail_copies, tails, table)
    total[...] = early_ref[...]
    used = list_blocks(table, small, BLOCKS, blocks)
    for copy in copies:
        copy.wait()
    block_sum(hidden_ref, weights, blocks, used, total)
    send_out(place_ref, total, sends, False)


def later_kernel(place_ref, gain_ref, *refs):
    bundles = refs[:SIDE]
    cells = refs[SIDE : SIDE + GRID_ROWS]
    sends = refs[SIDE + GRID_ROWS : 2 * SIDE + GRID_ROWS]
    normed, hidden, total_in, total_out = refs[2 * SIDE + GRID_ROWS : 2 * SIDE + GRID_ROWS + 4]
    work = refs[2 * SIDE + GRID_ROWS + 4 :]
    works = (work[: len(work) // 2], work[len(work) // 2 :])
    flights = []
    for k, (weights, tails, table, small, blocks, sems) in enumerate(works):
        flights.append(fetch(cells, k * SPAN, weights, tails, sems))
    for (tail_copies, _), (_, tails, table, _, _, _) in zip(flights, works):
        read_table(tail_copies, tails, table)
    squares = jnp.zeros((TOK, BLK), F32)
    for d in range(SIDE):
        for e in range(SIDE):
            for q in range(CHUNK):
                part = bundles[d][e, :, q * BLK : (q + 1) * BLK].astype(F32)
                squares = squares + part * part
    mean = jnp.sum(squares, axis=1, keepdims=True) / (BLOCKS * BLK)
    scale = lax.rsqrt(mean + EPSILON)
    for d in range(SIDE):
        for e in range(SIDE):
            chunk = chunk_of(place_ref, digit(place_ref[2] - d), e)
            for q in range(CHUNK):
                k = chunk * CHUNK + q
                part = bundles[d][e, :, q * BLK : (q + 1) * BLK].astype(F32)
                normed[k] = (part * scale * gain_ref[k]).astype(BF16)
    totals = (total_in, total_out)
    used = []
    for total, dummy, (_, _, table, small, blocks, _) in zip(totals, (FBL, BLOCKS), works):
        total[...] = jnp.zeros_like(total)
        used.append(list_blocks(table, small, dummy, blocks))
    for k, dense in enumerate((normed, hidden)):
        weights, _, _, _, blocks, _ = works[k]
        for copy in flights[k][1]:
            copy.wait()
        block_sum(dense, weights, blocks, used[k], totals[k])
        if k == 0:
            gelu_into(total_in, hidden)
    send_out(place_ref, total_out, sends, True)


def sum_of(refs, index):
    value = refs[0][index].astype(F32)
    for ref in refs[1:]:
        value = value + ref[index].astype(F32)
    return value


def whole_sum_kernel(*refs):
    for e in range(SIDE):
        refs[-1][e] = sum_of(refs[:-1], e).astype(refs[-1].dtype)


def merge_kernel(place_ref, *refs):
    bundle_ref, piece_ref = refs[-2:]
    for e in range(SIDE):
        bundle_ref[e] = sum_of(refs[:-2], e).astype(BF16)
    piece_ref[...] = bundle_ref[place_ref[3]]


def piece_sum_kernel(*refs):
    for e, piece in enumerate(refs[SIDE:]):
        piece[...] = sum_of(refs[:SIDE], e).astype(piece.dtype)


def cost(blocks, moved):
    return pl.CostEstimate(flops=blocks * 2 * BLK**3, bytes_accessed=moved, transcendentals=0)


def work(cells):
    return [
        pltpu.VMEM((cells * SLOTS * BLK, BLK), BF16),
        pltpu.VMEM((cells * TAIL, BLK), BF16),
        pltpu.VMEM((cells, BLK), jnp.int32),
        pltpu.SMEM((cells, BLK), jnp.int32),
        pltpu.SMEM((3, cells * SLOTS + 2 * SLOTS), jnp.int32),
        pltpu.SemaphoreType.DMA((2, cells)),
    ]


PARAMS = pltpu.CompilerParams(vmem_limit_bytes=16 << 20)
NORMED = jax.ShapeDtypeStruct((BLOCKS, TOK, BLK), BF16)
HIDDEN = jax.ShapeDtypeStruct((FBL, TOK, BLK), BF16)
BUNDLE = jax.ShapeDtypeStruct((SIDE, TOK, WIDTH), BF16)
PIECE = jax.ShapeDtypeStruct((TOK, WIDTH), BF16)


def first_norm(micro, place, inputs, gain):
    return pl.pallas_call(
        first_norm_kernel,
        grid_spec=pltpu.PrefetchScalarGridSpec(
            num_scalar_prefetch=2,
            grid=(1,),
            in_specs=[
                pl.BlockSpec((1, TOK, BLOCKS * BLK), lambda i, micro, place: (micro[0], 0, 0)),
                pl.BlockSpec((BLOCKS, 1, BLK), lambda i, micro, place: (0, 0, 0)),
            ],
            out_specs=[
                pl.BlockSpec((BLOCKS, TOK, BLK), lambda i, micro, place: (0, 0, 0)),
                pl.BlockSpec((SIDE, TOK, WIDTH), lambda i, micro, place: (0, 0, 0)),
            ],
        ),
        out_shape=[NORMED, BUNDLE],
        cost_estimate=cost(1, 6 << 20),
        compiler_params=PARAMS,
        name="first_norm",
    )(micro, place, inputs, gain)


def anywhere():
    return pl.BlockSpec(memory_space=pl.ANY)


def early_in(normed, cells):
    return pl.pallas_call(
        early_in_kernel,
        in_specs=[vmem()] + [anywhere()] * len(EARLY),
        out_specs=vmem(),
        out_shape=jax.ShapeDtypeStruct((FBL + 1, TOK, BLK), F32),
        scratch_shapes=work(len(EARLY)),
        cost_estimate=cost(384, 6 << 20),
        compiler_params=PARAMS,
        name="early_in",
    )(normed, *[cells[i] for i in EARLY])


def late_in(normed, early, cells):
    return pl.pallas_call(
        late_in_kernel,
        in_specs=[vmem()] * 2 + [anywhere()] * len(LATE),
        out_specs=vmem(),
        out_shape=HIDDEN,
        scratch_shapes=[pltpu.VMEM((FBL + 1, TOK, BLK), F32)] + work(len(LATE)),
        cost_estimate=cost(128, 3 << 20),
        compiler_params=PARAMS,
        name="late_in",
    )(normed, early, *[cells[i] for i in LATE])


def later_both(place, gain, bundles, cells):
    return pl.pallas_call(
        later_kernel,
        in_specs=[smem()] + [vmem()] * (1 + SIDE) + [anywhere()] * GRID_ROWS,
        out_specs=[vmem()] * SIDE,
        out_shape=[BUNDLE] * SIDE,
        scratch_shapes=[
            pltpu.VMEM((BLOCKS, TOK, BLK), BF16),
            pltpu.VMEM((FBL, TOK, BLK), BF16),
            pltpu.VMEM((FBL + 1, TOK, BLK), F32),
            pltpu.VMEM((BLOCKS + 1, TOK, BLK), F32),
        ]
        + work(GRID_ROWS)
        + work(GRID_ROWS),
        cost_estimate=cost(1024, 16 << 20),
        compiler_params=pltpu.CompilerParams(vmem_limit_bytes=24 << 20),
        name="later_both",
    )(place, gain, *bundles, *cells)


def early_out(hidden, cells):
    return pl.pallas_call(
        early_out_kernel,
        in_specs=[vmem()] + [anywhere()] * len(EARLY),
        out_specs=vmem(),
        out_shape=jax.ShapeDtypeStruct((BLOCKS + 1, TOK, BLK), F32),
        scratch_shapes=work(len(EARLY)),
        cost_estimate=cost(384, 6 << 20),
        compiler_params=PARAMS,
        name="early_out",
    )(hidden, *[cells[i] for i in EARLY])


def late_out(place, hidden, early, cells):
    return pl.pallas_call(
        late_out_kernel,
        in_specs=[smem()] + [vmem()] * 2 + [anywhere()] * len(LATE),
        out_specs=[vmem()] * SIDE,
        out_shape=[BUNDLE] * SIDE,
        scratch_shapes=[pltpu.VMEM((BLOCKS + 1, TOK, BLK), F32)] + work(len(LATE)),
        cost_estimate=cost(128, 6 << 20),
        compiler_params=PARAMS,
        name="late_out",
    )(place, hidden, early, *[cells[i] for i in LATE])


def pack(place, *sources):
    shape = jax.ShapeDtypeStruct((SPAN, BLK), BF16)
    return pl.pallas_call(
        pack_kernel,
        in_specs=[smem()] + [pl.BlockSpec(memory_space=pltpu.HBM)] * 6,
        out_specs=[vmem()] * 2,
        out_shape=[shape] * 2,
        scratch_shapes=[pltpu.SMEM((SLOTS,), jnp.int32)] * 2
        + [pltpu.SMEM((1,), jnp.int32)] * 2
        + [pltpu.SemaphoreType.DMA((6,))],
        cost_estimate=cost(0, 1 << 20),
        compiler_params=PARAMS,
        name="pack",
    )(place, *[pltpu.with_memory_space_constraint(v, pltpu.HBM) for v in sources[:4]], *sources[4:])


def add_up(kernel, place, bundles, outs):
    return pl.pallas_call(
        kernel,
        in_specs=([smem()] if place is not None else []) + [vmem()] * len(bundles),
        out_specs=[vmem()] * len(outs),
        out_shape=outs,
        cost_estimate=cost(0, 2 << 20),
        compiler_params=PARAMS,
    )(*([place] if place is not None else []), *bundles)


def on_rows(value, perm):
    return lax.ppermute(value, ("section", "row"), perm)


def on_cols(value, perm):
    return lax.ppermute(value, ("section", "col"), perm)


SWAP = [(i, (i + GRID_ROWS) % (2 * GRID_ROWS)) for i in range(2 * GRID_ROWS)]
AROUND = [(r, (r + 1) % GRID_ROWS) for r in range(GRID_ROWS)] + [
    (GRID_ROWS + r, GRID_ROWS + (r - 1) % GRID_ROWS) for r in range(GRID_ROWS)
]


def column_shift(first, distance):
    pairs = []
    for core in range(2):
        for y in range(SIDE):
            for x in range(SIDE):
                along_x = (core == 0) == first
                to_y = y if along_x else (y + distance) % SIDE
                to_x = (x + distance) % SIDE if along_x else x
                base = core * SIDE * SIDE
                pairs.append((base + y * SIDE + x, base + to_y * SIDE + to_x))
    return pairs


def ring_gather(cell):
    ring = [cell]
    other = []
    for step in range(1, GRID_ROWS // 2 + 1):
        ring.append(on_rows(ring[-1], AROUND))
        if step < GRID_ROWS // 2:
            other.append(on_rows(ring[-1], SWAP))
    return ring + other


def spread(values, first):
    landed = []
    for d in range(1, SIDE):
        value = values[d] if isinstance(values, (list, tuple)) else values
        landed.append(on_cols(value, column_shift(first, d)))
    return landed


def shards(inputs, norm_gain, w_in, w_in_slot, w_in_count, w_out, w_out_slot, w_out_count):
    core = lax.axis_index("section")
    row = lax.axis_index("row")
    col = lax.axis_index("col")
    y, x = col // SIDE, col % SIDE
    first = jnp.where(core == 0, x, y)
    second = jnp.where(core == 0, y, x)
    place = jnp.stack([core, col, first, second, row]).astype(jnp.int32)
    micro = jnp.reshape(core, (1,)).astype(jnp.int32)

    own_in, own_out = pack(
        place,
        w_in.reshape(SLOTS * BLK, BLK),
        w_out.reshape(SLOTS * BLK, BLK),
        w_in_slot.reshape(SLOTS),
        w_out_slot.reshape(SLOTS),
        w_in_count.reshape(1),
        w_out_count.reshape(1),
    )
    own_gain = norm_gain.reshape(BLOCKS, 1, BLK)
    other_in = on_rows(own_in, SWAP)
    other_out = on_rows(own_out, SWAP)
    other_gain = on_rows(own_gain, SWAP)
    mine = core == 0
    cells_in = ring_gather(jnp.where(mine, own_in, other_in))
    cells_out = ring_gather(jnp.where(mine, own_out, other_out))
    own_in, own_out, other_in, other_out, _ = lax.optimization_barrier(
        (own_in, own_out, other_in, other_out, cells_in[2])
    )
    later_cells = ring_gather(
        jnp.concatenate(
            [jnp.where(mine, other_in, own_in), jnp.where(mine, other_out, own_out)]
        ),
    )
    gains = [jnp.where(mine, own_gain, other_gain), jnp.where(mine, other_gain, own_gain)]

    normed, own_x = first_norm(micro, place, inputs, gains[0])
    early = early_in(normed, cells_in)
    hidden = late_in(normed, early, cells_in)
    early = early_out(hidden, cells_out)
    bundles = late_out(place, hidden, early, cells_out)
    landed = spread(bundles, True)
    sums = add_up(whole_sum_kernel, None, [bundles[0]] + landed, [BUNDLE])[0]
    landed = spread(sums, False)
    base = add_up(
        whole_sum_kernel, None, [own_x, sums], [jax.ShapeDtypeStruct(BUNDLE.shape, F32)]
    )[0]
    middle, piece = add_up(merge_kernel, place, [base] + landed, [BUNDLE, PIECE])

    bundles = [middle] + spread(middle, True)
    bundles = later_both(place, gains[1], bundles, later_cells)
    landed = spread(bundles, True)
    sums = add_up(
        piece_sum_kernel,
        None,
        [bundles[0]] + landed,
        [jax.ShapeDtypeStruct((TOK, WIDTH), F32)] + [PIECE] * (SIDE - 1),
    )
    total = sums[0]
    for value in spread(sums, False):
        total = total + value.astype(F32)
    final = (piece.astype(F32) + total).astype(BF16)

    other = on_rows(jnp.where(mine, final, piece), SWAP)
    return jnp.stack([jnp.where(mine, piece, other), jnp.where(mine, other, final)])[None]


def solution(mesh):
    placed = (
        P(None, "row", None),
        P("section", None),
        P("section", "row", "col", None, None, None),
        P("section", "row", "col", None),
        P("section", "row", "col"),
        P("section", "row", "col", None, None, None),
        P("section", "row", "col", None),
        P("section", "row", "col"),
    )

    return jax.shard_map(
        shards,
        mesh=mesh,
        in_specs=placed,
        out_specs=P("section", None, "row", "col"),
        check_vma=False,
    )
```

```python
import jax
import jax.numpy as jnp
from jax import lax
from jax.experimental import pallas as pl
from jax.experimental.pallas import tpu as pltpu
from jax.sharding import PartitionSpec as P


EPSILON = 1e-05
BLK = 128
SLOTS = 8
UNROLL = 8
TAIL = 16
SPAN = 1024 + TAIL
GRID_ROWS = 8
SIDE = 4
DBL = 6
FBL = 12
BLOCKS = 48
CHUNK = 3
TOK = 128
WIDTH = CHUNK * BLK


F32 = jnp.float32
BF16 = jnp.bfloat16


def vmem():
    return pl.BlockSpec(memory_space=pltpu.VMEM)


def smem():
    return pl.BlockSpec(memory_space=pltpu.SMEM)


def chunk_of(place_ref, first, second):
    core = place_ref[0]
    return jnp.where(core == 0, second * SIDE + first, first * SIDE + second)


def digit(value):
    return lax.rem(value + 2 * SIDE, SIDE)


def pack_kernel(place_ref, *refs):
    sources, outs, slots, counts, sems = refs[:6], refs[6:8], refs[8:10], refs[10:12], refs[12]
    small = [
        pltpu.make_async_copy(source, target, sems.at[2 + k])
        for k, (source, target) in enumerate(zip(sources[2:], slots + counts))
    ]
    copies = [
        pltpu.make_async_copy(sources[k], outs[k].at[pl.ds(0, SLOTS * BLK)], sems.at[k])
        for k in range(2)
    ]
    for copy in small + copies:
        copy.start()
    for copy in small:
        copy.wait()
    lane = lax.broadcasted_iota(jnp.int32, (TAIL, BLK), 1)
    for k, out in enumerate(outs):
        row = jnp.where(lane == 2 * SLOTS, counts[k][0], 0)
        for n in range(SLOTS):
            slot = slots[k][n]
            model, hid = place_ref[4] * DBL + slot // FBL, lax.rem(slot, FBL)
            row = jnp.where(lane == n, hid if k else model, row)
            row = jnp.where(lane == SLOTS + n, model if k else hid, row)
        out[SLOTS * BLK : SPAN, :] = row.astype(F32).astype(BF16)
    for copy in copies:
        copy.wait()


def fetch(cells, offset, weights, tails, sems):
    size = SLOTS * BLK
    copies = []
    for i, cell in enumerate(cells):
        copies.append(
            pltpu.make_async_copy(
                cell.at[pl.ds(offset + size, TAIL)], tails.at[pl.ds(i * TAIL, TAIL)], sems.at[1, i]
            )
        )
    for i, cell in enumerate(cells):
        copies.append(
            pltpu.make_async_copy(
                cell.at[pl.ds(offset, size)], weights.at[pl.ds(i * size, size)], sems.at[0, i]
            )
        )
    for copy in copies:
        copy.start()
    return copies[:GRID_ROWS], copies[GRID_ROWS:]


def read_table(copies, tails, table):
    for copy in copies:
        copy.wait()
    for i in range(GRID_ROWS):
        rows = tails[i * TAIL : (i + 1) * TAIL, :].astype(F32).astype(jnp.int32)
        table[i : i + 1, :] = rows[0:1, :]


def list_blocks(table, small, dummy, blocks):
    pltpu.sync_copy(table, small)
    used = 0
    for i in range(GRID_ROWS):
        for n in range(SLOTS):
            blocks[0, used + n] = i * SLOTS + n
            blocks[1, used + n] = small[i, n]
            blocks[2, used + n] = small[i, SLOTS + n]
        used = used + small[i, 2 * SLOTS]
    for n in range(UNROLL):
        blocks[0, used + n] = 0
        blocks[1, used + n] = 0
        blocks[2, used + n] = dummy
    return used


def block_sum(dense, weights, blocks, used, total):
    def group(step, carry):
        at = step * UNROLL
        products = [
            jnp.dot(
                dense[blocks[1, at + u]],
                weights[pl.ds(pl.multiple_of(blocks[0, at + u] * BLK, BLK), BLK), :],
                preferred_element_type=F32,
            )
            for u in range(UNROLL)
        ]
        for u, product in enumerate(products):
            total[blocks[2, at + u]] += product
        return carry

    lax.fori_loop(0, (used + UNROLL - 1) // UNROLL, group, 0)


def gelu_into(total, hidden):
    for f in range(FBL):
        hidden[f] = jax.nn.gelu(total[f], approximate=True).astype(BF16)


def first_norm_kernel(micro_ref, place_ref, x_ref, gain_ref, normed_ref, own_ref):
    squares = jnp.zeros((TOK, BLK), F32)
    for k in range(BLOCKS):
        part = x_ref[0, :, k * BLK : (k + 1) * BLK].astype(F32)
        squares = squares + part * part
    mean = jnp.sum(squares, axis=1, keepdims=True) / (BLOCKS * BLK)
    scale = lax.rsqrt(mean + EPSILON)
    for k in range(BLOCKS):
        part = x_ref[0, :, k * BLK : (k + 1) * BLK].astype(F32)
        normed_ref[k] = (part * scale * gain_ref[k]).astype(BF16)
    for e in range(SIDE):
        start = pl.multiple_of(chunk_of(place_ref, place_ref[2], e) * WIDTH, BLK)
        own_ref[e] = x_ref[0, :, pl.ds(start, WIDTH)]


def first_in_kernel(normed_ref, *refs):
    cells = refs[:GRID_ROWS]
    hidden_ref, total, weights, tails, table, small, blocks, sems = refs[GRID_ROWS:]
    tail_copies, copies = fetch(cells, 0, weights, tails, sems)
    read_table(tail_copies, tails, table)
    total[...] = jnp.zeros_like(total)
    used = list_blocks(table, small, FBL, blocks)
    for copy in copies:
        copy.wait()
    block_sum(normed_ref, weights, blocks, used, total)
    gelu_into(total, hidden_ref)


def send_out(place_ref, total, sends, relative):
    for d in range(SIDE):
        for e in range(SIDE):
            second = digit(place_ref[3] + e) if relative else e
            chunk = chunk_of(place_ref, digit(place_ref[2] + d), second)
            for q in range(CHUNK):
                sends[d][e, :, q * BLK : (q + 1) * BLK] = total[chunk * CHUNK + q].astype(BF16)


def first_out_kernel(place_ref, hidden_ref, *refs):
    cells = refs[:GRID_ROWS]
    sends = refs[GRID_ROWS : GRID_ROWS + SIDE]
    total, weights, tails, table, small, blocks, sems = refs[GRID_ROWS + SIDE :]
    tail_copies, copies = fetch(cells, 0, weights, tails, sems)
    read_table(tail_copies, tails, table)
    total[...] = jnp.zeros_like(total)
    used = list_blocks(table, small, BLOCKS, blocks)
    for copy in copies:
        copy.wait()
    block_sum(hidden_ref, weights, blocks, used, total)
    send_out(place_ref, total, sends, False)


def later_kernel(place_ref, gain_ref, *refs):
    bundles = refs[:SIDE]
    cells = refs[SIDE : SIDE + GRID_ROWS]
    sends = refs[SIDE + GRID_ROWS : 2 * SIDE + GRID_ROWS]
    normed, hidden, total_in, total_out = refs[2 * SIDE + GRID_ROWS : 2 * SIDE + GRID_ROWS + 4]
    work = refs[2 * SIDE + GRID_ROWS + 4 :]
    works = (work[: len(work) // 2], work[len(work) // 2 :])
    flights = []
    for k, (weights, tails, table, small, blocks, sems) in enumerate(works):
        flights.append(fetch(cells, k * SPAN, weights, tails, sems))
    for (tail_copies, _), (_, tails, table, _, _, _) in zip(flights, works):
        read_table(tail_copies, tails, table)
    squares = jnp.zeros((TOK, BLK), F32)
    for d in range(SIDE):
        for e in range(SIDE):
            for q in range(CHUNK):
                part = bundles[d][e, :, q * BLK : (q + 1) * BLK].astype(F32)
                squares = squares + part * part
    mean = jnp.sum(squares, axis=1, keepdims=True) / (BLOCKS * BLK)
    scale = lax.rsqrt(mean + EPSILON)
    for d in range(SIDE):
        for e in range(SIDE):
            chunk = chunk_of(place_ref, digit(place_ref[2] - d), e)
            for q in range(CHUNK):
                k = chunk * CHUNK + q
                part = bundles[d][e, :, q * BLK : (q + 1) * BLK].astype(F32)
                normed[k] = (part * scale * gain_ref[k]).astype(BF16)
    totals = (total_in, total_out)
    used = []
    for total, dummy, (_, _, table, small, blocks, _) in zip(totals, (FBL, BLOCKS), works):
        total[...] = jnp.zeros_like(total)
        used.append(list_blocks(table, small, dummy, blocks))
    for k, dense in enumerate((normed, hidden)):
        weights, _, _, _, blocks, _ = works[k]
        for copy in flights[k][1]:
            copy.wait()
        block_sum(dense, weights, blocks, used[k], totals[k])
        if k == 0:
            gelu_into(total_in, hidden)
    send_out(place_ref, total_out, sends, True)


def sum_of(refs, index):
    value = refs[0][index].astype(F32)
    for ref in refs[1:]:
        value = value + ref[index].astype(F32)
    return value


def whole_sum_kernel(*refs):
    for e in range(SIDE):
        refs[-1][e] = sum_of(refs[:-1], e).astype(BF16)


def merge_kernel(place_ref, *refs):
    bundle_ref, piece_ref = refs[-2:]
    for e in range(SIDE):
        bundle_ref[e] = sum_of(refs[:-2], e).astype(BF16)
    piece_ref[...] = bundle_ref[place_ref[3]]


def piece_sum_kernel(*refs):
    for e, piece in enumerate(refs[SIDE:]):
        piece[...] = sum_of(refs[:SIDE], e).astype(piece.dtype)


def cost(blocks, moved):
    return pl.CostEstimate(flops=blocks * 2 * BLK**3, bytes_accessed=moved, transcendentals=0)


WORK = [
    pltpu.VMEM((GRID_ROWS * SLOTS * BLK, BLK), BF16),
    pltpu.VMEM((GRID_ROWS * TAIL, BLK), BF16),
    pltpu.VMEM((GRID_ROWS, BLK), jnp.int32),
    pltpu.SMEM((GRID_ROWS, BLK), jnp.int32),
    pltpu.SMEM((3, GRID_ROWS * SLOTS + 2 * SLOTS), jnp.int32),
    pltpu.SemaphoreType.DMA((2, GRID_ROWS)),
]
PARAMS = pltpu.CompilerParams(vmem_limit_bytes=16 << 20)
NORMED = jax.ShapeDtypeStruct((BLOCKS, TOK, BLK), BF16)
HIDDEN = jax.ShapeDtypeStruct((FBL, TOK, BLK), BF16)
BUNDLE = jax.ShapeDtypeStruct((SIDE, TOK, WIDTH), BF16)
PIECE = jax.ShapeDtypeStruct((TOK, WIDTH), BF16)


def first_norm(micro, place, inputs, gain):
    return pl.pallas_call(
        first_norm_kernel,
        grid_spec=pltpu.PrefetchScalarGridSpec(
            num_scalar_prefetch=2,
            grid=(1,),
            in_specs=[
                pl.BlockSpec((1, TOK, BLOCKS * BLK), lambda i, micro, place: (micro[0], 0, 0)),
                pl.BlockSpec((BLOCKS, 1, BLK), lambda i, micro, place: (0, 0, 0)),
            ],
            out_specs=[
                pl.BlockSpec((BLOCKS, TOK, BLK), lambda i, micro, place: (0, 0, 0)),
                pl.BlockSpec((SIDE, TOK, WIDTH), lambda i, micro, place: (0, 0, 0)),
            ],
        ),
        out_shape=[NORMED, BUNDLE],
        cost_estimate=cost(1, 6 << 20),
        compiler_params=PARAMS,
        name="first_norm",
    )(micro, place, inputs, gain)


def anywhere():
    return pl.BlockSpec(memory_space=pl.ANY)


def first_in(normed, cells):
    return pl.pallas_call(
        first_in_kernel,
        in_specs=[vmem()] + [anywhere()] * GRID_ROWS,
        out_specs=vmem(),
        out_shape=HIDDEN,
        scratch_shapes=[pltpu.VMEM((FBL + 1, TOK, BLK), F32)] + WORK,
        cost_estimate=cost(512, 8 << 20),
        compiler_params=PARAMS,
        name="first_in",
    )(normed, *cells)


def later_both(place, gain, bundles, cells):
    return pl.pallas_call(
        later_kernel,
        in_specs=[smem()] + [vmem()] * (1 + SIDE) + [anywhere()] * GRID_ROWS,
        out_specs=[vmem()] * SIDE,
        out_shape=[BUNDLE] * SIDE,
        scratch_shapes=[
            pltpu.VMEM((BLOCKS, TOK, BLK), BF16),
            pltpu.VMEM((FBL, TOK, BLK), BF16),
            pltpu.VMEM((FBL + 1, TOK, BLK), F32),
            pltpu.VMEM((BLOCKS + 1, TOK, BLK), F32),
        ]
        + WORK
        + WORK,
        cost_estimate=cost(1024, 16 << 20),
        compiler_params=pltpu.CompilerParams(vmem_limit_bytes=24 << 20),
        name="later_both",
    )(place, gain, *bundles, *cells)


def project_out(place, hidden, cells):
    return pl.pallas_call(
        first_out_kernel,
        in_specs=[smem(), vmem()] + [anywhere()] * GRID_ROWS,
        out_specs=[vmem()] * SIDE,
        out_shape=[BUNDLE] * SIDE,
        scratch_shapes=[pltpu.VMEM((BLOCKS + 1, TOK, BLK), F32)] + WORK,
        cost_estimate=cost(512, 8 << 20),
        compiler_params=PARAMS,
        name="project_out",
    )(place, hidden, *cells)


def pack(place, *sources):
    shape = jax.ShapeDtypeStruct((SPAN, BLK), BF16)
    return pl.pallas_call(
        pack_kernel,
        in_specs=[smem()] + [pl.BlockSpec(memory_space=pltpu.HBM)] * 6,
        out_specs=[vmem()] * 2,
        out_shape=[shape] * 2,
        scratch_shapes=[pltpu.SMEM((SLOTS,), jnp.int32)] * 2
        + [pltpu.SMEM((1,), jnp.int32)] * 2
        + [pltpu.SemaphoreType.DMA((6,))],
        cost_estimate=cost(0, 1 << 20),
        compiler_params=PARAMS,
        name="pack",
    )(place, *[pltpu.with_memory_space_constraint(v, pltpu.HBM) for v in sources[:4]], *sources[4:])


def add_up(kernel, place, bundles, outs):
    return pl.pallas_call(
        kernel,
        in_specs=([smem()] if place is not None else []) + [vmem()] * len(bundles),
        out_specs=[vmem()] * len(outs),
        out_shape=outs,
        cost_estimate=cost(0, 2 << 20),
        compiler_params=PARAMS,
    )(*([place] if place is not None else []), *bundles)


def on_rows(value, perm):
    return lax.ppermute(value, ("section", "row"), perm)


def on_cols(value, perm):
    return lax.ppermute(value, ("section", "col"), perm)


SWAP = [(i, (i + GRID_ROWS) % (2 * GRID_ROWS)) for i in range(2 * GRID_ROWS)]
AROUND = [(r, (r + 1) % GRID_ROWS) for r in range(GRID_ROWS)] + [
    (GRID_ROWS + r, GRID_ROWS + (r - 1) % GRID_ROWS) for r in range(GRID_ROWS)
]


def column_shift(first, distance):
    pairs = []
    for core in range(2):
        for y in range(SIDE):
            for x in range(SIDE):
                along_x = (core == 0) == first
                to_y = y if along_x else (y + distance) % SIDE
                to_x = (x + distance) % SIDE if along_x else x
                base = core * SIDE * SIDE
                pairs.append((base + y * SIDE + x, base + to_y * SIDE + to_x))
    return pairs


def ring_gather(cell):
    ring = [cell]
    other = []
    for step in range(1, GRID_ROWS // 2 + 1):
        ring.append(on_rows(ring[-1], AROUND))
        if step < GRID_ROWS // 2:
            other.append(on_rows(ring[-1], SWAP))
    return ring + other


def spread(values, first):
    landed = []
    for d in range(1, SIDE):
        value = values[d] if isinstance(values, (list, tuple)) else values
        landed.append(on_cols(value, column_shift(first, d)))
    return landed


def shards(inputs, norm_gain, w_in, w_in_slot, w_in_count, w_out, w_out_slot, w_out_count):
    core = lax.axis_index("section")
    row = lax.axis_index("row")
    col = lax.axis_index("col")
    y, x = col // SIDE, col % SIDE
    first = jnp.where(core == 0, x, y)
    second = jnp.where(core == 0, y, x)
    place = jnp.stack([core, col, first, second, row]).astype(jnp.int32)
    micro = jnp.reshape(core, (1,)).astype(jnp.int32)

    own_in, own_out = pack(
        place,
        w_in.reshape(SLOTS * BLK, BLK),
        w_out.reshape(SLOTS * BLK, BLK),
        w_in_slot.reshape(SLOTS),
        w_out_slot.reshape(SLOTS),
        w_in_count.reshape(1),
        w_out_count.reshape(1),
    )
    own_gain = norm_gain.reshape(BLOCKS, 1, BLK)
    other_in = on_rows(own_in, SWAP)
    other_out = on_rows(own_out, SWAP)
    other_gain = on_rows(own_gain, SWAP)
    mine = core == 0
    cells_in = ring_gather(jnp.where(mine, own_in, other_in))
    cells_out = ring_gather(jnp.where(mine, own_out, other_out))
    own_in, own_out, other_in, other_out, _ = lax.optimization_barrier(
        (own_in, own_out, other_in, other_out, cells_in[2])
    )
    later_cells = ring_gather(
        jnp.concatenate(
            [jnp.where(mine, other_in, own_in), jnp.where(mine, other_out, own_out)]
        ),
    )
    gains = [jnp.where(mine, own_gain, other_gain), jnp.where(mine, other_gain, own_gain)]

    normed, own_x = first_norm(micro, place, inputs, gains[0])
    hidden = first_in(normed, cells_in)
    bundles = project_out(place, hidden, cells_out)
    landed = spread(bundles, True)
    sums = add_up(whole_sum_kernel, None, [bundles[0]] + landed, [BUNDLE])[0]
    landed = spread(sums, False)
    middle, piece = add_up(merge_kernel, place, [own_x, sums] + landed, [BUNDLE, PIECE])

    bundles = [middle] + spread(middle, True)
    bundles = later_both(place, gains[1], bundles, later_cells)
    landed = spread(bundles, True)
    sums = add_up(
        piece_sum_kernel,
        None,
        [bundles[0]] + landed,
        [jax.ShapeDtypeStruct((TOK, WIDTH), F32)] + [PIECE] * (SIDE - 1),
    )
    total = sums[0]
    for value in spread(sums, False):
        total = total + value.astype(F32)
    final = (piece.astype(F32) + total).astype(BF16)

    other = on_rows(jnp.where(mine, final, piece), SWAP)
    return jnp.stack([jnp.where(mine, piece, other), jnp.where(mine, other, final)])[None]


def solution(mesh):
    placed = (
        P(None, "row", None),
        P("section", None),
        P("section", "row", "col", None, None, None),
        P("section", "row", "col", None),
        P("section", "row", "col"),
        P("section", "row", "col", None, None, None),
        P("section", "row", "col", None),
        P("section", "row", "col"),
    )

    return jax.shard_map(
        shards,
        mesh=mesh,
        in_specs=placed,
        out_specs=P("section", None, "row", "col"),
        check_vma=False,
    )
```
